32 devices in a mesh: groups: 2 (over x), rows: 16 (over z, y, core).
Axes of the slice: x: 2, y: 2, z: 4, core: 2. Of those that a mesh axis runs over, the one named last changes fastest.
Arguments:
- token_ids: int32 [1, 256], P(None, 'groups'), parts along dimension 1, may hold values from 0 to 32767
- parents: int32 [1, 8, 32], P(None, 'groups'), parts along dimension 1, may hold values from 0 to 31, as said below
- states: bfloat16 [256, 16, 128, 128], P(('groups', 'rows')), parts along dimension 0, may hold values from -1.75 to 1.75
- embed_table: bfloat16 [32768, 2048], P(None, 'rows'), may hold values from -6 to 6
- qkv_weight: bfloat16 [2048, 3, 2048], P(None, None, 'rows'), may hold values from -0.125 to 0.125
- gate_weight: float32 [16, 128], replicated, may hold values from -6 to 6
- gate_bias: float32 [16], replicated, may hold values from -2 to 3
- norm_gain: float32 [2048], replicated, may hold values from 0.1 to 1.9
- out_weight: bfloat16 [2048, 2048], P(None, 'rows'), may hold values from -0.125 to 0.125
Outputs:
- layer_out: bfloat16 [1, 256, 2048], P(None, 'groups', 'rows'), parts along dimension 1
- final_states: bfloat16 [256, 16, 128, 128], P(('groups', 'rows')), parts along dimension 0
The draws below stay inside these ranges and needn't reach their ends.
There are 2 independent parts, one for each index of `groups`. The reference program is written for one: setup_inputs(seed, part) draws one part's arguments, and reference() takes and returns one part's arrays. A program takes and returns all parts, laid end to end along the dimension named above; an argument that names none is the same for every part. Nothing has to cross between parts.
Inputs may be any that keep to these rules, and one draw needn't show every extreme that they name: The 32 beams of a user fall into 4 aligned blocks of 8. In every step and for every user, at most 2 children of one block have parents in any one other block, and in every step some user has exactly 2 children of one block with parents in another block.
All inputs are finite; a program needn't handle non-finite values.
Results may differ from the reference program's by a relative error of at most 0.0074.
Values may be sent and summed in bfloat16 or wider, within the bound.
A program may use at most 64 MiB of HBM per device.

```python
import math
import jax
import jax.numpy as jnp
import numpy as np
from jax import lax

HEADS = 16
HEAD = 128
VOCAB = 32768
BEAM = 32
CAP = 2
STEPS = 1
D = 2048
R_ALL = 128
USERS = 4


def draw_parents(key, part):
    key_list = jax.random.split(jax.random.fold_in(key, 11), 6)
    row_count = BEAM // 4
    shape_four = (STEPS, USERS, 4, row_count)
    counts = jax.random.randint(key_list[0], (STEPS, USERS, 4, 3), 0, CAP + 1)
    pick_dev = jax.random.randint(key_list[1], (STEPS, USERS, 1, 1), 0, 4)
    pick_off = jax.random.randint(key_list[2], (STEPS, USERS, 1, 1), 0, 3)
    dev_index = jnp.arange(4, dtype=jnp.int32)[None, None, :, None]
    off_index = jnp.arange(3, dtype=jnp.int32)[None, None, None, :]
    counts = jnp.where((dev_index == pick_dev) & (off_index == pick_off), CAP, counts)
    limits = jnp.cumsum(counts, axis=-1)
    slot_index = jnp.arange(row_count, dtype=jnp.int32)[None, None, None, :]
    offset = jnp.where(slot_index < limits[..., 0:1], 1, jnp.where(slot_index < limits[..., 1:2], 2, jnp.where(slot_index < limits[..., 2:3], 3, 0)))
    scores = jax.random.randint(key_list[3], shape_four, 0, 1 << 20) * row_count + slot_index
    ordering = jnp.argsort(scores, axis=-1, stable=True)
    offset = jnp.take_along_axis(offset, ordering, axis=-1)
    source = jnp.bitwise_xor(dev_index, offset)
    first_draw = jax.random.randint(key_list[4], shape_four, 0, row_count)
    second = jax.random.randint(key_list[5], shape_four, 0, row_count)
    within = jnp.minimum(first_draw, second)
    return (source * row_count + within).reshape(STEPS, USERS, BEAM).astype(jnp.int32)


def place_ends(array, rng, low, top_value):
    place = [jax.random.randint(jax.random.fold_in(rng, axis), (), 0, length) for axis, length in enumerate(array.shape)]
    main_axis = array.shape.index(max(array.shape))
    neighbour = place[:main_axis] + [(place[main_axis] + 1) % array.shape[main_axis]] + place[main_axis + 1:]
    return array.at[tuple(place)].set(low).at[tuple(neighbour)].set(top_value)


def block_levels(key, dims, shards, smallest, largest):
    level, own = 1.0, jax.random.fold_in(key, 6)
    for axis_at, parts in shards:
        steps = jnp.exp(jax.random.uniform(jax.random.fold_in(own, axis_at), (parts,), jnp.float32, smallest / len(shards), largest / len(shards)))
        level = level * jnp.repeat(steps, dims[axis_at] // parts).reshape([-1 if axis == axis_at else 1 for axis in range(len(dims))])
    return level


def cumulative_ranks(number_of, skew):
    loads = [(1 << 20) // math.isqrt(rank ** skew) + 1 for rank in range(1, number_of + 1)]
    scale = 1 + sum(loads) // (1 << 30)
    return np.cumsum(np.array([max(1, weight // scale) for weight in loads]))


def ranked(own_key, extent, amount, lean):
    grid = cumulative_ranks(amount, lean)
    lot = jax.random.randint(jax.random.fold_in(own_key, 1), extent, 0, int(grid[amount - 1]))
    rank = jnp.searchsorted(jnp.asarray(grid, jnp.int32), lot, side="right")
    return jax.random.permutation(jax.random.fold_in(own_key, 2), amount)[rank].astype(jnp.int32)


def scatter_about(stream_key, dims, spread, reach, shards=(), held_as=jnp.bfloat16):
    array = spread * jax.random.normal(stream_key, dims, jnp.float32)
    if shards:
        array = array * block_levels(stream_key, dims, shards, -0.22, 0.18)
    return jnp.clip(array, -reach, reach).astype(held_as)


def setup_inputs(seed: int = 0, part: int = 0) -> dict:
    seeds = jax.random.split(jax.random.key(seed), 10)
    part_splits = jax.random.split(jax.random.fold_in(seeds[9], part), 10)
    token_ids = place_ends(ranked(part_splits[0], (STEPS, R_ALL), VOCAB, 2), jax.random.fold_in(part_splits[0], 3), 0, VOCAB - 1).astype(jnp.int32)
    parents = draw_parents(jax.random.fold_in(jax.random.fold_in(seeds[9], part), 71), part)
    states = scatter_about(part_splits[2], (R_ALL, HEADS, HEAD, HEAD), 0.3, 1.75, ((0, 16),))
    embed_table = scatter_about(seeds[3], (VOCAB, D), 1.0, 6.0, ((1, 16),))
    qkv_weight = scatter_about(seeds[4], (D, 3, D), D ** -0.5, 0.125, ((2, 16),))
    gate_weight = scatter_about(seeds[5], (HEADS, HEAD), 1.0, 6.0, (), jnp.float32)
    gate_bias = jnp.clip(jax.random.uniform(seeds[6], (HEADS,), jnp.float32, -2.0, 3.0), -2.0, 3.0)
    norm_gain = jnp.clip(1.0 + 0.18 * jax.random.normal(seeds[7], (D,), jnp.float32), 0.1, 1.9)
    out_weight = scatter_about(seeds[8], (D, D), D ** -0.5, 0.125, ((1, 16),))
    return {"token_ids": token_ids, "parents": parents, "states": states, "embed_table": embed_table, "qkv_weight": qkv_weight, "gate_weight": gate_weight, "gate_bias": gate_bias, "norm_gain": norm_gain, "out_weight": out_weight}


def reference(token_ids, parents, states, embed_table, qkv_weight, gate_weight, gate_bias, norm_gain, out_weight):
    width = HEADS * HEAD
    row_count = USERS * BEAM
    weight_flat = qkv_weight.reshape(width, 3 * width)
    state_now = states
    outputs = []
    for step_index in range(STEPS):
        inputs = jnp.take(embed_table, token_ids[step_index], axis=0)
        projected = jnp.dot(inputs, weight_flat, preferred_element_type=jnp.float32).astype(jnp.bfloat16)
        projected = projected.reshape(row_count, 3, HEADS, HEAD)
        parent_rows = (jnp.arange(USERS, dtype=jnp.int32)[:, None] * BEAM + parents[step_index]).reshape(row_count)
        prior_state = jnp.take(state_now, parent_rows, axis=0)

        def update(block):
            prior_block, proj_block = block
            queries = proj_block[:, 0].astype(jnp.float32)
            key_float = proj_block[:, 1].astype(jnp.float32)
            values = proj_block[:, 2].astype(jnp.float32)
            gate_logit = lax.optimization_barrier(jnp.sum(key_float * gate_weight, axis=-1)) / math.sqrt(HEAD) + gate_bias
            decay_rate = jax.nn.sigmoid(gate_logit)
            key_unit = key_float * lax.rsqrt(lax.optimization_barrier(jnp.sum(key_float * key_float, axis=-1, keepdims=True)) + 1e-06)
            new_state = decay_rate[:, :, None, None] * prior_block.astype(jnp.float32) + key_unit[:, :, :, None] * values[:, :, None, :]
            new_state = new_state.astype(jnp.bfloat16)
            readout = jnp.einsum('bhd,bhde->bhe', queries, new_state.astype(jnp.float32))
            scaled = readout * lax.rsqrt(lax.optimization_barrier(jnp.mean(readout * readout, axis=-1, keepdims=True)) + 1e-05)
            normed = (scaled.reshape(BEAM, width) * norm_gain).astype(jnp.bfloat16)
            return (new_state, normed)
        new_states, normed = lax.map(update, (prior_state.reshape(USERS, BEAM, HEADS, HEAD, HEAD), projected.reshape(USERS, BEAM, 3, HEADS, HEAD)))
        state_now = new_states.reshape(row_count, HEADS, HEAD, HEAD)
        attention = jnp.dot(normed.reshape(row_count, width), out_weight, preferred_element_type=jnp.float32)
        outputs.append((inputs.astype(jnp.float32) + attention).astype(jnp.bfloat16))
    return (jnp.stack(outputs), state_now)
```

```python
import functools
import math

import jax
import jax.numpy as jnp
from jax import lax
from jax.experimental import pallas as pl
from jax.experimental.pallas import tpu as pltpu
from jax.sharding import PartitionSpec as P

CAP = 2
ANY = pl.BlockSpec(memory_space=pl.ANY)
VM = pl.BlockSpec(memory_space=pltpu.VMEM)
SM = pl.BlockSpec(memory_space=pltpu.SMEM)


def pack_kernel(chosen_ref, state_ref, one_ref, two_ref, three_ref, buf, in_sem, out_sem):
    outs = (one_ref, two_ref, three_ref)
    order = [2, 3, 4, 5, 0, 1]
    loads = {}
    for slot in order:
        loads[slot] = pltpu.make_async_copy(
            state_ref.at[chosen_ref[slot]], buf.at[slot], in_sem.at[slot]
        )
        loads[slot].start()
    stores = []
    for slot in order:
        loads[slot].wait()
        store = pltpu.make_async_copy(
            buf.at[slot], outs[slot // CAP].at[slot % CAP], out_sem.at[slot]
        )
        store.start()
        stores.append(store)
    for store in stores:
        store.wait()


def pack(chosen, states):
    block = jax.ShapeDtypeStruct((CAP,) + states.shape[1:], states.dtype)
    count = 3 * CAP
    size = count * math.prod(states.shape[1:]) * 2
    return pl.pallas_call(
        pack_kernel,
        out_shape=(block, block, block),
        in_specs=[SM, ANY],
        out_specs=(ANY, ANY, ANY),
        scratch_shapes=[
            pltpu.VMEM((count,) + states.shape[1:], states.dtype),
            pltpu.SemaphoreType.DMA((count,)),
            pltpu.SemaphoreType.DMA((count,)),
        ],
        cost_estimate=pl.CostEstimate(flops=0, bytes_accessed=2 * size, transcendentals=0),
        name="pack_states",
    )(chosen, states)


def embed_kernel(tok_ref, table_ref, out_ref, buf, wide, rows_out, sem):
    count = out_ref.shape[0]

    def begin(i, _):
        pltpu.make_async_copy(table_ref.at[tok_ref[i] // 8], buf.at[i], sem).start()
        return _

    lax.fori_loop(0, count, begin, 0, unroll=8)
    pltpu.make_async_copy(table_ref.at[pl.ds(0, count)], buf, sem).wait()
    wide[...] = buf[...].astype(jnp.float32).reshape(wide.shape)

    def pick(i, _):
        rows_out[pl.ds(i, 1), :] = wide[pl.ds(i * 8 + tok_ref[i] % 8, 1), :]
        return _

    lax.fori_loop(0, count, pick, 0, unroll=8)
    out_ref[...] = rows_out[...].astype(jnp.bfloat16)


def embed(tokens, table):
    count, width = tokens.shape[0], table.shape[1]
    return pl.pallas_call(
        embed_kernel,
        out_shape=jax.ShapeDtypeStruct((count, width), table.dtype),
        in_specs=[SM, ANY],
        out_specs=VM,
        scratch_shapes=[
            pltpu.VMEM((count, 8, width), table.dtype),
            pltpu.VMEM((count * 8, width), jnp.float32),
            pltpu.VMEM((count, width), jnp.float32),
            pltpu.SemaphoreType.DMA,
        ],
        cost_estimate=pl.CostEstimate(
            flops=0, bytes_accessed=count * 8 * width * 2, transcendentals=0
        ),
        name="embed_rows",
    )(tokens, table.reshape(table.shape[0] // 8, 8, width))


def greet(peers):
    barrier = pltpu.get_barrier_semaphore()
    for peer in peers:
        pl.semaphore_signal(
            barrier, inc=1, device_id={"rows": peer}, device_id_type=pl.DeviceIdType.MESH
        )
    pl.semaphore_wait(barrier, len(peers))


def spread_kernel(count, spans, mode, in_ref, out_ref, send_sem, recv_sem, own_sem):
    me = lax.axis_index("rows")
    level = count // 4
    member = me % 4
    my_level = me // 4
    side = my_level * 4 + (member + 2) % 4
    twin = my_level * 4 + member + 1 - 2 * (member % 2)
    side_twin = my_level * 4 + (twin % 4 + 2) % 4
    peers = [((my_level + k) % level) * 4 + member for k in range(1, level)]
    side_peers = [((my_level + k) % level) * 4 + (member + 2) % 4 for k in range(1, level)]

    def place(block):
        if mode == "columns":
            return out_ref.at[:, pl.ds(pl.multiple_of(block * spans, spans), spans)]
        return out_ref.at[pl.ds(pl.multiple_of(block * spans, spans), spans)]

    sent = []

    def send(source, block, target):
        copy = pltpu.make_async_remote_copy(
            src_ref=source,
            dst_ref=place(block),
            send_sem=send_sem.at[len(sent)],
            recv_sem=recv_sem.at[block],
            device_id={"rows": target},
            device_id_type=pl.DeviceIdType.MESH,
        )
        copy.start()
        sent.append(copy)

    def arrived(block):
        pltpu.make_async_remote_copy(
            src_ref=place(block),
            dst_ref=place(block),
            send_sem=send_sem.at[0],
            recv_sem=recv_sem.at[block],
            device_id={"rows": twin},
            device_id_type=pl.DeviceIdType.MESH,
        ).wait_recv()

    greet([side, twin] + peers)
    if mode == "exchange":
        def part(owner):
            return in_ref.at[pl.ds(pl.multiple_of(owner * spans, spans), spans)]

        for peer in reversed(peers):
            send(part(peer // 4), me, peer)
        mine = part(my_level)
        send(mine, me, side)
        send(mine, me, twin)
        own = pltpu.make_async_copy(mine, place(me), own_sem)
        own.start()
        for peer in peers:
            arrived(peer)
            send(place(peer), peer, side)
            send(place(peer), peer, twin)
        arrived(side)
        send(place(side), side, twin)
        for peer in side_peers:
            arrived(peer)
            send(place(peer), peer, twin)
    else:
        send(in_ref, me, side)
        for peer in peers:
            send(in_ref, me, peer)
        send(in_ref, me, twin)
        own = pltpu.make_async_copy(in_ref, place(me), own_sem)
        own.start()
        arrived(side)
        for peer in peers:
            send(place(side), side, peer)
        send(place(side), side, twin)
        for k in range(level - 1):
            arrived(peers[k])
            send(place(peers[k]), peers[k], twin)
        for k in range(level - 1):
            arrived(side_peers[k])
            send(place(side_peers[k]), side_peers[k], twin)
    arrived(twin)
    arrived(side_twin)
    for k in range(1, level):
        base = ((my_level + k) % level) * 4
        arrived(base + twin % 4)
        arrived(base + side_twin % 4)
    own.wait()
    for copy in sent:
        copy.wait_send()


def spread(block, count, spans, mode, out_shape, identity, name):
    return pl.pallas_call(
        functools.partial(spread_kernel, count, spans, mode),
        out_shape=jax.ShapeDtypeStruct(out_shape, block.dtype),
        in_specs=[VM],
        out_specs=VM,
        scratch_shapes=[
            pltpu.SemaphoreType.DMA((count - 1,)),
            pltpu.SemaphoreType.DMA((count,)),
            pltpu.SemaphoreType.DMA,
        ],
        compiler_params=pltpu.CompilerParams(collective_id=identity, has_side_effects=True),
        cost_estimate=pl.CostEstimate(
            flops=0, bytes_accessed=16 * math.prod(out_shape), transcendentals=0
        ),
        name=name,
    )(block)


def read_kernel(
    head_size, bias_ref, qkv_ref, state_ref, weight_ref, gain_ref, owner_ref, slot_ref, out_ref
):
    head = pl.program_id(0)
    block = qkv_ref[0]
    queries = block[:, :head_size].astype(jnp.float32)
    keys = block[:, head_size : 2 * head_size].astype(jnp.float32)
    values = block[:, 2 * head_size :].astype(jnp.float32)
    logit = jnp.sum(keys * weight_ref[0], axis=-1, keepdims=True) / math.sqrt(head_size)
    decay = jax.nn.sigmoid(logit + bias_ref[head])
    unit = keys * lax.rsqrt(jnp.sum(keys * keys, axis=-1, keepdims=True) + 1e-06)
    total = jnp.zeros(queries.shape, jnp.float32)
    for parent in range(state_ref.shape[0]):
        chosen = (queries * owner_ref[:, parent : parent + 1]).astype(jnp.bfloat16)
        total += jnp.dot(chosen, state_ref[parent, 0], preferred_element_type=jnp.float32)
    readout = decay * total + jnp.sum(queries * unit, axis=-1, keepdims=True) * values
    scaled = readout * lax.rsqrt(jnp.mean(readout * readout, axis=-1, keepdims=True) + 1e-05)
    normed = (scaled * gain_ref[0]).astype(jnp.bfloat16)
    out_ref[...] = jnp.dot(slot_ref[...], normed, preferred_element_type=jnp.float32).astype(
        jnp.bfloat16
    )


def read(qkv, states, gate_weight, gate_bias, norm_gain, owner, slot_pick):
    heads, beams, triple = qkv.shape
    row_local, _, head_size, _ = states.shape
    slots = slot_pick.shape[0]
    return pl.pallas_call(
        functools.partial(read_kernel, head_size),
        grid=(heads,),
        out_shape=jax.ShapeDtypeStruct((slots, heads * head_size), jnp.bfloat16),
        in_specs=[
            SM,
            pl.BlockSpec((1, beams, triple), lambda h: (h, 0, 0)),
            pl.BlockSpec((row_local, 1, head_size, head_size), lambda h: (0, h, 0, 0)),
            pl.BlockSpec((1, 1, head_size), lambda h: (h, 0, 0)),
            pl.BlockSpec((1, 1, head_size), lambda h: (h, 0, 0)),
            pl.BlockSpec((beams, row_local), lambda h: (0, 0)),
            pl.BlockSpec((slots, beams), lambda h: (0, 0)),
        ],
        out_specs=pl.BlockSpec((slots, head_size), lambda h: (0, h)),
        cost_estimate=pl.CostEstimate(
            flops=2 * beams * math.prod(states.shape),
            bytes_accessed=2 * math.prod(states.shape),
            transcendentals=0,
        ),
        name="read_heads",
    )(
        gate_bias,
        qkv,
        states,
        gate_weight.reshape(heads, 1, head_size),
        norm_gain.reshape(heads, 1, head_size),
        owner,
        slot_pick,
    )


def update_kernel(
    kind_ref, index_ref, decay_ref, state_ref, one_ref, two_ref, three_ref, unit_ref, value_ref,
    out_ref, old, new, in_sem, out_sem
):
    row_local, heads = old.shape[0], old.shape[1]
    sources = (state_ref, one_ref, two_ref, three_ref)
    for row in range(row_local):
        for kind, source in enumerate(sources):
            @pl.when(kind_ref[row] == kind)
            def _():
                pltpu.make_async_copy(
                    source.at[index_ref[row]], old.at[row], in_sem.at[row]
                ).start()

    def step(row, carry):
        pltpu.make_async_copy(state_ref.at[0], old.at[row], in_sem.at[row]).wait()
        columns = unit_ref[row]
        values = value_ref[row]
        for head in range(heads):
            fresh = columns[:, head : head + 1] * values[head : head + 1, :]
            prior = old[row, head].astype(jnp.float32)
            new[row, head] = (decay_ref[row, head] * prior + fresh).astype(jnp.bfloat16)
        pltpu.make_async_copy(new.at[row], out_ref.at[row], out_sem.at[row]).start()
        return carry

    lax.fori_loop(0, row_local, step, 0)
    for row in range(row_local):
        pltpu.make_async_copy(new.at[row], out_ref.at[row], out_sem.at[row]).wait()


def update(kind, index, decay, states, one, two, three, unit, values):
    row_local = states.shape[0]
    return pl.pallas_call(
        update_kernel,
        out_shape=jax.ShapeDtypeStruct(states.shape, states.dtype),
        in_specs=[SM, SM, SM, ANY, ANY, ANY, ANY, VM, VM],
        out_specs=ANY,
        scratch_shapes=[
            pltpu.VMEM(states.shape, states.dtype),
            pltpu.VMEM(states.shape, states.dtype),
            pltpu.SemaphoreType.DMA((row_local,)),
            pltpu.SemaphoreType.DMA((row_local,)),
        ],
        cost_estimate=pl.CostEstimate(
            flops=4 * math.prod(states.shape),
            bytes_accessed=4 * math.prod(states.shape),
            transcendentals=0,
        ),
        name="update_states",
    )(kind, index, decay, states, one, two, three, unit, values)


def swap(block, partner):
    count = lax.axis_size("rows")
    return lax.ppermute(block, "rows", [(low, low ^ partner) for low in range(count)])


def fast(
    token_ids, parents, states, embed_table, qkv_weight, gate_weight, gate_bias, norm_gain,
    out_weight
):
    row_local, heads, head_size, _ = states.shape
    width = heads * head_size
    column_local = embed_table.shape[1]
    row_total = token_ids.shape[1]
    users, beams = parents.shape[1], parents.shape[2]
    count = lax.axis_size("rows")
    device = lax.axis_index("rows")
    member, user = device % 4, device // 4
    slots = 16 * ((row_local + 3 * CAP + 15) // 16)

    lists = parents[0]
    owner_block = lists // row_local
    blocks = owner_block.reshape(users, 4, row_local)
    at = jnp.arange(row_local, dtype=jnp.int32)
    same = (blocks[..., :, None] == blocks[..., None, :]) & (at[:, None] > at[None, :])
    rank = jnp.sum(same.astype(jnp.int32), axis=-1)
    offset = jnp.bitwise_xor(blocks, jnp.arange(4, dtype=jnp.int32)[None, :, None])
    slot = jnp.where(offset == 0, at[None, None, :], row_local + (offset - 1) * CAP + rank)
    slot = slot.reshape(users, beams)
    my_list = lax.dynamic_index_in_dim(lists, user, 0, keepdims=False)
    my_slot = lax.dynamic_index_in_dim(slot, user, 0, keepdims=False)
    held = my_list // row_local == member
    within = my_list % row_local
    slot_pick = held[None, :] & (my_slot[None, :] == jnp.arange(slots, dtype=jnp.int32)[:, None])
    chosen = jnp.sum(
        jnp.where(slot_pick[row_local : row_local + 3 * CAP], within[None, :], 0), axis=1
    )
    owner = (held[:, None] & (within[:, None] == at[None, :])).astype(jnp.float32)
    own_slot = lax.dynamic_slice_in_dim(my_slot, member * row_local, row_local, 0)
    own_within = lax.dynamic_slice_in_dim(within, member * row_local, row_local, 0)
    far = own_slot >= row_local
    kind = jnp.where(far, (own_slot - row_local) // CAP + 1, 0)
    index = jnp.where(far, (own_slot - row_local) % CAP, own_within)

    one, two, three = pack(chosen, states)
    got_two = swap(two, 2)
    got_three = swap(three, 3)
    got_one = swap(one, 1)

    local_columns = embed(token_ids[0], embed_table)
    every_input = spread(
        local_columns, count, column_local, "columns", (row_total, count * column_local), 1,
        "spread_inputs"
    )
    projected = jnp.dot(
        every_input,
        qkv_weight.reshape(qkv_weight.shape[0], 3 * column_local),
        preferred_element_type=jnp.float32,
    ).astype(jnp.bfloat16)
    qkv = spread(
        projected.reshape(row_total, 3 * column_local), count, beams, "exchange",
        (count * beams, 3 * column_local), 2, "spread_heads"
    ).reshape(count, beams, 3 * column_local)
    normed = read(
        qkv, states, gate_weight, gate_bias, norm_gain, owner, slot_pick.astype(jnp.bfloat16)
    )
    every_normed = spread(
        normed, count, slots, "rows", (count * slots, width), 3, "spread_normed"
    )
    source = (
        (jnp.arange(users, dtype=jnp.int32)[:, None] * 4 + owner_block) * slots + slot
    ).reshape(row_total)
    pick = (source[:, None] == jnp.arange(count * slots, dtype=jnp.int32)[None, :]).astype(
        jnp.bfloat16
    )
    ordered = jnp.dot(pick, every_normed, preferred_element_type=jnp.float32)
    attention = jnp.dot(
        ordered.astype(jnp.bfloat16), out_weight, preferred_element_type=jnp.float32
    )
    layer_out = (local_columns.astype(jnp.float32) + attention).astype(jnp.bfloat16)

    mine = lax.dynamic_slice_in_dim(qkv, member * row_local, row_local, 1)
    keys = mine[:, :, head_size : 2 * head_size].astype(jnp.float32)
    values = jnp.swapaxes(mine[:, :, 2 * head_size :].astype(jnp.float32), 0, 1)
    logit = jnp.sum(keys * gate_weight[:, None, :], axis=-1) / math.sqrt(head_size)
    decay = jax.nn.sigmoid(logit + gate_bias[:, None]).T
    unit = keys * lax.rsqrt(jnp.sum(keys * keys, axis=-1, keepdims=True) + 1e-06)
    state_now = update(
        kind, index, decay, states, got_one, got_two, got_three, jnp.transpose(unit, (1, 2, 0)),
        values
    )
    return (layer_out[None], state_now)


def from_partner(block, axis, stride):
    count = lax.axis_size(axis)
    route = []
    for low in range(count):
        high = low | 1 << stride
        if high != low and high < count:
            route += [(low, high), (high, low)]
    return lax.ppermute(block, axis, route)


def outgoing(state_now, parent_list, member, row_local, partner):
    target = jnp.bitwise_xor(member, partner)
    children = lax.dynamic_slice_in_dim(parent_list, target * row_local, row_local, 0)
    needed = children // row_local == member
    rank_index = jnp.cumsum(needed.astype(jnp.int32)) - 1
    slot_ids = jnp.arange(CAP, dtype=jnp.int32)
    chosen = jnp.sum(
        jnp.where(
            needed[None, :] & (rank_index[None, :] == slot_ids[:, None]),
            (children % row_local)[None, :],
            0,
        ),
        axis=1,
    )
    return jnp.take(state_now, chosen, axis=0)


def route(state_now, parent_list, member, row_local):
    first_out = outgoing(state_now, parent_list, member, row_local, 1)
    second_out = outgoing(state_now, parent_list, member, row_local, 2)
    corner_out = outgoing(state_now, parent_list, member, row_local, 3)
    got_one = from_partner(first_out, "rows", 0)
    got_two = from_partner(second_out, "rows", 1)
    relayed = from_partner(corner_out, "rows", 0)
    got_three = from_partner(relayed, "rows", 1)
    own_list = lax.dynamic_slice_in_dim(parent_list, member * row_local, row_local, 0)
    source = own_list // row_local
    partner = jnp.bitwise_xor(source, member)
    slot_index = jnp.arange(row_local, dtype=jnp.int32)
    earlier = (source[:, None] == source[None, :]) & (slot_index[:, None] > slot_index[None, :])
    rank_index = jnp.sum(earlier.astype(jnp.int32), axis=1)
    position = jnp.where(
        partner == 0, own_list % row_local, row_local + (partner - 1) * CAP + rank_index
    )
    pooled = jnp.concatenate([state_now, got_one, got_two, got_three], 0)
    return jnp.take(pooled, position, axis=0)


def per_device(
    token_ids,
    parents,
    states,
    embed_table,
    qkv_weight,
    gate_weight,
    gate_bias,
    norm_gain,
    out_weight,
):
    row_local = states.shape[0]
    heads = states.shape[1]
    head_size = states.shape[2]
    count = lax.axis_size("rows")
    if (
        embed_table.shape[1] == head_size
        and head_size % 128 == 0
        and count == heads
        and parents.shape[0] == 1
        and parents.shape[2] == 4 * row_local
        and parents.shape[1] * 4 == count
        and parents.shape[2] % 16 == 0
    ):
        return fast(
            token_ids, parents, states, embed_table, qkv_weight, gate_weight, gate_bias,
            norm_gain, out_weight
        )
    width = heads * head_size
    column_local = embed_table.shape[1]
    row_total = token_ids.shape[1]
    device = lax.axis_index("rows")
    member = device % 4
    user_index = device // 4
    weight_flat = qkv_weight.reshape(qkv_weight.shape[0], 3 * column_local)
    local_columns = jnp.take(embed_table, token_ids, axis=0)
    every_proj = jnp.einsum(
        "...rc,cf->...rf",
        lax.all_gather(local_columns, "rows", axis=2, tiled=True),
        weight_flat,
        preferred_element_type=jnp.float32,
    )
    state_now = states
    step_proj = every_proj[0]
    projected = step_proj.astype(jnp.bfloat16).reshape(row_total, 3, column_local)
    mine = lax.all_to_all(projected, "rows", split_axis=0, concat_axis=2, tiled=True)
    queries = mine[:, 0].reshape(row_local, heads, head_size)
    key_float = mine[:, 1].reshape(row_local, heads, head_size).astype(jnp.float32)
    values = mine[:, 2].reshape(row_local, heads, head_size).astype(jnp.float32)
    gate_logit = jnp.sum(key_float * gate_weight, axis=-1) / math.sqrt(head_size) + gate_bias
    decay_rate = jax.nn.sigmoid(gate_logit)
    key_unit = key_float * lax.rsqrt(jnp.sum(key_float * key_float, axis=-1, keepdims=True) + 1e-06)
    parent_list = lax.dynamic_index_in_dim(parents[0], user_index, 0, keepdims=False)
    prior_state = route(state_now, parent_list, member, row_local)
    new_state = (
        decay_rate[:, :, None, None] * prior_state.astype(jnp.float32)
        + key_unit[:, :, :, None] * values[:, :, None, :]
    )
    state_now = new_state.astype(jnp.bfloat16)
    readout = jnp.einsum("rhd,rhde->rhe", queries, state_now, preferred_element_type=jnp.float32)
    scaled = readout * lax.rsqrt(jnp.mean(readout * readout, axis=-1, keepdims=True) + 1e-05)
    normed = (scaled.reshape(row_local, width) * norm_gain).astype(jnp.bfloat16)
    attention = jnp.dot(
        lax.all_gather(normed, "rows", axis=0, tiled=True),
        out_weight,
        preferred_element_type=jnp.float32,
    )
    outputs = [(local_columns[0].astype(jnp.float32) + attention).astype(jnp.bfloat16)]
    return (jnp.stack(outputs), state_now)


def solution(mesh):
    placed = (
        P(None, "groups"),
        P(None, "groups", None),
        P(("groups", "rows"), None, None, None),
        P(None, "rows"),
        P(None, None, "rows"),
        P(),
        P(),
        P(),
        P(None, "rows"),
    )
    return jax.shard_map(
        per_device,
        mesh=mesh,
        in_specs=placed,
        out_specs=(P(None, "groups", "rows"), P(("groups", "rows"), None, None, None)),
        check_vma=False,
    )
```

```python
import functools
import math

import jax
import jax.numpy as jnp
from jax import lax
from jax.experimental import pallas as pl
from jax.experimental.pallas import tpu as pltpu
from jax.sharding import PartitionSpec as P

CAP = 2
ANY = pl.BlockSpec(memory_space=pl.ANY)
VM = pl.BlockSpec(memory_space=pltpu.VMEM)
SM = pl.BlockSpec(memory_space=pltpu.SMEM)


def gather_kernel(
    level, list_ref, tok_ref, state_ref, table_ref, one_ref, far_ref, out_ref,
    buf, rows_in, wide, rows_out, in_sem, out_sem, row_sem
):
    device = lax.axis_index("rows")
    member, user = device % 4, device // 4
    row_local = state_ref.shape[0]
    loads = []
    for slot in list(range(CAP, 3 * CAP)) + list(range(CAP)):
        partner, order = slot // CAP + 1, slot % CAP
        base = jnp.bitwise_xor(member, partner) * row_local
        seen, chosen = jnp.int32(0), jnp.int32(0)
        for child in range(row_local):
            parent = list_ref[0, user, base + child]
            needed = parent // row_local == member
            chosen = jnp.where(needed & (seen == order), parent % row_local, chosen)
            seen = seen + needed.astype(jnp.int32)
        load = pltpu.make_async_copy(state_ref.at[chosen], buf.at[slot], in_sem.at[slot])
        load.start()
        loads.append((slot, load))
    count = out_ref.shape[0]

    def begin(i, carry):
        pltpu.make_async_copy(table_ref.at[tok_ref[0, i] // 8], rows_in.at[i], row_sem).start()
        return carry

    lax.fori_loop(0, count, begin, 0, unroll=8)
    stores = []
    for slot, load in loads:
        load.wait()
        target = one_ref.at[slot] if slot < CAP else far_ref.at[slot - CAP]
        store = pltpu.make_async_copy(buf.at[slot], target, out_sem.at[slot])
        store.start()
        stores.append(store)
    pltpu.make_async_copy(table_ref.at[pl.ds(0, count)], rows_in, row_sem).wait()
    wide[...] = rows_in[...].astype(jnp.float32).reshape(wide.shape)

    def pick(i, carry):
        rows_out[pl.ds(i, 1), :] = wide[pl.ds(i * 8 + tok_ref[0, i] % 8, 1), :]
        return carry

    lax.fori_loop(0, count, pick, 0, unroll=8)
    out_ref[...] = rows_out[...].astype(jnp.bfloat16)
    for store in stores:
        store.wait()


def gather(parents, tokens, states, table):
    rest = states.shape[1:]
    slots = 3 * CAP
    count, width = tokens.shape[1], table.shape[1]
    size = slots * math.prod(rest) * 2
    return pl.pallas_call(
        functools.partial(gather_kernel, parents.shape[1]),
        out_shape=(
            jax.ShapeDtypeStruct((CAP,) + rest, states.dtype),
            jax.ShapeDtypeStruct((2 * CAP,) + rest, states.dtype),
            jax.ShapeDtypeStruct((count, width), table.dtype),
        ),
        in_specs=[SM, SM, ANY, ANY],
        out_specs=(ANY, ANY, VM),
        scratch_shapes=[
            pltpu.VMEM((slots,) + rest, states.dtype),
            pltpu.VMEM((count, 8, width), table.dtype),
            pltpu.VMEM((count * 8, width), jnp.float32),
            pltpu.VMEM((count, width), jnp.float32),
            pltpu.SemaphoreType.DMA((slots,)),
            pltpu.SemaphoreType.DMA((slots,)),
            pltpu.SemaphoreType.DMA,
        ],
        cost_estimate=pl.CostEstimate(flops=0, bytes_accessed=2 * size, transcendentals=0),
        name="gather_rows",
    )(parents, tokens, states, table.reshape(table.shape[0] // 8, 8, width))


def greet(peers):
    barrier = pltpu.get_barrier_semaphore()
    for peer in peers:
        pl.semaphore_signal(
            barrier, inc=1, device_id={"rows": peer}, device_id_type=pl.DeviceIdType.MESH
        )
    pl.semaphore_wait(barrier, len(peers))


def spread_kernel(count, spans, mode, first, heads, near, *refs):
    refs = list(refs)
    in_ref, far_ref = refs[0], refs[1]
    one_ref = refs.pop(2) if near else None
    out_ref, got_ref = refs[2], refs[3]
    got_one_ref = refs.pop(4) if near else None
    stage, send_sem, recv_sem, own_sem, bulk_send, bulk_recv = refs[4:]
    me = lax.axis_index("rows")
    level = count // 4
    member = me % 4
    my_level = me // 4
    side_member = (member + 2) % 4
    twin_member = member + 1 - 2 * (member % 2)
    diag_member = (twin_member + 2) % 4
    side = my_level * 4 + side_member
    twin = my_level * 4 + twin_member
    diag = my_level * 4 + diag_member
    levels = [(my_level + k) % level for k in range(1, level)]
    peers = [other * 4 + member for other in levels]
    side_peers = [other * 4 + side_member for other in levels]

    def place(block):
        if mode == "columns":
            return out_ref.at[:, pl.ds(pl.multiple_of(block * spans, spans), spans)]
        return out_ref.at[pl.ds(pl.multiple_of(block * spans, spans), spans)]

    def part(ref, other):
        if mode == "exchange":
            return ref.at[pl.ds(pl.multiple_of(other * spans, spans), spans)]
        return ref

    def remote(source, target_ref, out_sem, in_sem, target):
        return pltpu.make_async_remote_copy(
            src_ref=source,
            dst_ref=target_ref,
            send_sem=out_sem,
            recv_sem=in_sem,
            device_id={"rows": target},
            device_id_type=pl.DeviceIdType.MESH,
        )

    sent = []

    def send(source, block, target, target_ref=None):
        target_ref = place(block) if target_ref is None else target_ref
        copy = remote(source, target_ref, send_sem.at[len(sent)], recv_sem.at[block], target)
        copy.start()
        sent.append(copy)

    def arrived(block, ref=None):
        ref = place(block) if ref is None else ref
        remote(ref, ref, send_sem.at[0], recv_sem.at[block], twin).wait_recv()

    greet([side, twin, diag] + peers)
    landing = stage if mode == "exchange" else place(side)
    send(in_ref, me, side, stage if mode == "exchange" else None)
    bulk = []
    for slot in range(2 * CAP):
        bulk.append(
            remote(
                far_ref.at[slot, pl.ds(first, heads)],
                got_ref.at[slot],
                bulk_send.at[slot],
                bulk_recv.at[slot],
                side if slot < CAP else diag,
            )
        )
    if near:
        bulk.append(
            remote(
                one_ref, got_one_ref, bulk_send.at[2 * CAP], bulk_recv.at[2 * CAP], twin
            )
        )
    for other in levels:
        send(part(in_ref, other), me, other * 4 + member)
    send(part(in_ref, my_level), me, twin)
    for copy in bulk:
        copy.start()
    own = pltpu.make_async_copy(part(in_ref, my_level), place(me), own_sem.at[0])
    own.start()
    arrived(side, landing)
    for other in levels:
        send(part(landing, other), side, other * 4 + member)
    send(part(landing, my_level), side, twin)
    if mode == "exchange":
        extra = pltpu.make_async_copy(part(stage, my_level), place(side), own_sem.at[1])
        extra.start()
    for peer in peers + side_peers:
        arrived(peer)
        send(place(peer), peer, twin)
    arrived(twin)
    arrived(diag)
    for other in levels:
        arrived(other * 4 + twin_member)
        arrived(other * 4 + diag_member)
    own.wait()
    if mode == "exchange":
        extra.wait()
    for copy in sent:
        copy.wait_send()
    for copy in bulk:
        copy.wait()


def spread(block, far, one, count, spans, mode, first, heads, out_shape, identity, name):
    near = one is not None
    got = jax.ShapeDtypeStruct((far.shape[0], heads) + far.shape[2:], far.dtype)
    outs = (jax.ShapeDtypeStruct(out_shape, block.dtype), got)
    operands = (block, far)
    if near:
        outs = outs + (jax.ShapeDtypeStruct(one.shape, one.dtype),)
        operands = operands + (one,)
    return pl.pallas_call(
        functools.partial(spread_kernel, count, spans, mode, first, heads, near),
        out_shape=outs,
        in_specs=[VM] + [ANY] * (len(operands) - 1),
        out_specs=(VM,) + (ANY,) * (len(outs) - 1),
        scratch_shapes=[
            pltpu.VMEM(block.shape if mode == "exchange" else (16, 128), block.dtype),
            pltpu.SemaphoreType.DMA((count - 1,)),
            pltpu.SemaphoreType.DMA((count,)),
            pltpu.SemaphoreType.DMA((2,)),
            pltpu.SemaphoreType.DMA((2 * CAP + 1,)),
            pltpu.SemaphoreType.DMA((2 * CAP + 1,)),
        ],
        compiler_params=pltpu.CompilerParams(collective_id=identity, has_side_effects=True),
        name=name,
    )(*operands)


def read_kernel(
    head_size, bias_ref, qkv_ref, state_ref, weight_ref, gain_ref, owner_ref, slot_ref, out_ref
):
    step = pl.program_id(0)
    group = qkv_ref.shape[0]
    masks = [owner_ref[:, p : p + 1] > 0 for p in range(state_ref.shape[0])]
    for head in range(group):
        block = qkv_ref[head]
        q_half = block[:, :head_size]
        queries = q_half.astype(jnp.float32)
        keys = block[:, head_size : 2 * head_size].astype(jnp.float32)
        values = block[:, 2 * head_size :].astype(jnp.float32)
        logit = jnp.sum(keys * weight_ref[head], axis=-1, keepdims=True) / math.sqrt(head_size)
        decay = jax.nn.sigmoid(logit + bias_ref[step * group + head])
        unit = keys * lax.rsqrt(jnp.sum(keys * keys, axis=-1, keepdims=True) + 1e-06)
        spreadq = jnp.concatenate(
            [jnp.where(mask, queries, 0.0).astype(jnp.bfloat16) for mask in masks], axis=1
        )
        stacked = state_ref[:, head].reshape(state_ref.shape[0] * head_size, head_size)
        total = jnp.dot(spreadq, stacked, preferred_element_type=jnp.float32)
        readout = decay * total + jnp.sum(queries * unit, axis=-1, keepdims=True) * values
        scaled = readout * lax.rsqrt(jnp.mean(readout * readout, axis=-1, keepdims=True) + 1e-05)
        normed = (scaled * gain_ref[head]).astype(jnp.bfloat16)
        picked = jnp.dot(slot_ref[...], normed, preferred_element_type=jnp.float32)
        out_ref[:, head * head_size : (head + 1) * head_size] = picked.astype(jnp.bfloat16)


def read(qkv, states, gate_weight, gate_bias, norm_gain, owner, slot_pick):
    heads, beams, triple = qkv.shape
    row_local, _, head_size, _ = states.shape
    slots = slot_pick.shape[0]
    group = 4 if heads % 4 == 0 else 1
    return pl.pallas_call(
        functools.partial(read_kernel, head_size),
        grid=(heads // group,),
        out_shape=jax.ShapeDtypeStruct((slots, heads * head_size), jnp.bfloat16),
        in_specs=[
            SM,
            pl.BlockSpec((group, beams, triple), lambda h: (h, 0, 0)),
            pl.BlockSpec((row_local, group, head_size, head_size), lambda h: (0, h, 0, 0)),
            pl.BlockSpec((group, 1, head_size), lambda h: (h, 0, 0)),
            pl.BlockSpec((group, 1, head_size), lambda h: (h, 0, 0)),
            pl.BlockSpec((beams, row_local), lambda h: (0, 0)),
            pl.BlockSpec((slots, beams), lambda h: (0, 0)),
        ],
        out_specs=pl.BlockSpec((slots, group * head_size), lambda h: (0, h)),
        cost_estimate=pl.CostEstimate(
            flops=2 * beams * math.prod(states.shape),
            bytes_accessed=2 * math.prod(states.shape),
            transcendentals=0,
        ),
        name="read_heads",
    )(
        gate_bias,
        qkv,
        states,
        gate_weight.reshape(heads, 1, head_size),
        norm_gain.reshape(heads, 1, head_size),
        owner,
        slot_pick,
    )


def update_kernel(cuts, kind_ref, index_ref, decay_ref, state_ref, one_ref, *refs):
    pieces = refs[: len(cuts)]
    unit_ref, value_ref, out_ref, old, new, in_sem, out_sem = refs[len(cuts) :]
    row_local, heads = old.shape[0], old.shape[1]
    for row in range(row_local):
        @pl.when(kind_ref[row] == 0)
        def _():
            pltpu.make_async_copy(
                state_ref.at[index_ref[row]], old.at[row], in_sem.at[row]
            ).start()

        @pl.when(kind_ref[row] == 1)
        def _():
            pltpu.make_async_copy(one_ref.at[index_ref[row]], old.at[row], in_sem.at[row]).start()

        @pl.when(kind_ref[row] > 1)
        def _():
            slot = (kind_ref[row] - 2) * CAP + index_ref[row]
            for (first, span), piece in zip(cuts, pieces):
                pltpu.make_async_copy(
                    piece.at[slot], old.at[row, pl.ds(first, span)], in_sem.at[row]
                ).start()

    def step(row, carry):
        pltpu.make_async_copy(state_ref.at[0], old.at[row], in_sem.at[row]).wait()
        columns = unit_ref[row]
        values = value_ref[row]
        for head in range(heads):
            fresh = columns[:, head : head + 1] * values[head : head + 1, :]
            prior = old[row, head].astype(jnp.float32)
            new[row, head] = (decay_ref[row, head] * prior + fresh).astype(jnp.bfloat16)
        pltpu.make_async_copy(new.at[row], out_ref.at[row], out_sem.at[row]).start()
        return carry

    lax.fori_loop(0, row_local, step, 0)
    for row in range(row_local):
        pltpu.make_async_copy(new.at[row], out_ref.at[row], out_sem.at[row]).wait()


def update(cuts, kind, index, decay, states, one, pieces, unit, values):
    row_local = states.shape[0]
    return pl.pallas_call(
        functools.partial(update_kernel, cuts),
        out_shape=jax.ShapeDtypeStruct(states.shape, states.dtype),
        in_specs=[SM, SM, SM, ANY, ANY] + [ANY] * len(pieces) + [VM, VM],
        out_specs=ANY,
        scratch_shapes=[
            pltpu.VMEM(states.shape, states.dtype),
            pltpu.VMEM(states.shape, states.dtype),
            pltpu.SemaphoreType.DMA((row_local,)),
            pltpu.SemaphoreType.DMA((row_local,)),
        ],
        cost_estimate=pl.CostEstimate(
            flops=4 * math.prod(states.shape),
            bytes_accessed=4 * math.prod(states.shape),
            transcendentals=0,
        ),
        name="update_states",
    )(kind, index, decay, states, one, *pieces, unit, values)


def fast(
    token_ids, parents, states, embed_table, qkv_weight, gate_weight, gate_bias, norm_gain,
    out_weight
):
    row_local, heads, head_size, _ = states.shape
    width = heads * head_size
    column_local = embed_table.shape[1]
    row_total = token_ids.shape[1]
    users, beams = parents.shape[1], parents.shape[2]
    count = lax.axis_size("rows")
    device = lax.axis_index("rows")
    member, user = device % 4, device // 4
    slots = 16 * ((row_local + 3 * CAP + 15) // 16)

    lists = parents[0]
    owner_block = lists // row_local
    blocks = owner_block.reshape(users, 4, row_local)
    at = jnp.arange(row_local, dtype=jnp.int32)
    same = (blocks[..., :, None] == blocks[..., None, :]) & (at[:, None] > at[None, :])
    rank = jnp.sum(same.astype(jnp.int32), axis=-1)
    offset = jnp.bitwise_xor(blocks, jnp.arange(4, dtype=jnp.int32)[None, :, None])
    slot = jnp.where(offset == 0, at[None, None, :], row_local + (offset - 1) * CAP + rank)
    slot = slot.reshape(users, beams)
    my_list = lax.dynamic_index_in_dim(lists, user, 0, keepdims=False)
    my_slot = lax.dynamic_index_in_dim(slot, user, 0, keepdims=False)
    held = my_list // row_local == member
    within = my_list % row_local
    slot_pick = held[None, :] & (my_slot[None, :] == jnp.arange(slots, dtype=jnp.int32)[:, None])
    owner = (held[:, None] & (within[:, None] == at[None, :])).astype(jnp.float32)
    own_slot = lax.dynamic_slice_in_dim(my_slot, member * row_local, row_local, 0)
    own_within = lax.dynamic_slice_in_dim(within, member * row_local, row_local, 0)
    far = own_slot >= row_local
    kind = jnp.where(far, (own_slot - row_local) // CAP + 1, 0)
    index = jnp.where(far, (own_slot - row_local) % CAP, own_within)

    edges = [0, heads * 3 // 16, heads * 8 // 16, heads]
    cuts = tuple((low, high - low) for low, high in zip(edges, edges[1:]))
    one, far, local_columns = gather(parents, token_ids, states, embed_table)
    every_input, piece_a = spread(
        local_columns, far, None, count, column_local, "columns", *cuts[0],
        (row_total, count * column_local), 1, "spread_inputs"
    )
    projected = jnp.dot(
        every_input,
        qkv_weight.reshape(qkv_weight.shape[0], 3 * column_local),
        preferred_element_type=jnp.float32,
    ).astype(jnp.bfloat16)
    qkv, piece_b, got_one = spread(
        projected.reshape(row_total, 3 * column_local), far, one, count, beams, "exchange",
        *cuts[1], (count * beams, 3 * column_local), 2, "spread_heads"
    )
    qkv = qkv.reshape(count, beams, 3 * column_local)
    normed = read(
        qkv, states, gate_weight, gate_bias, norm_gain, owner, slot_pick.astype(jnp.bfloat16)
    )
    every_normed, piece_c = spread(
        normed, far, None, count, slots, "rows", *cuts[2], (count * slots, width), 3,
        "spread_normed"
    )
    source = (
        (jnp.arange(users, dtype=jnp.int32)[:, None] * 4 + owner_block) * slots + slot
    ).reshape(row_total)
    pick = (source[:, None] == jnp.arange(count * slots, dtype=jnp.int32)[None, :]).astype(
        jnp.bfloat16
    )
    ordered = jnp.dot(pick, every_normed, preferred_element_type=jnp.float32)
    attention = jnp.dot(
        ordered.astype(jnp.bfloat16), out_weight, preferred_element_type=jnp.float32
    )
    layer_out = (local_columns.astype(jnp.float32) + attention).astype(jnp.bfloat16)

    mine = lax.dynamic_slice_in_dim(qkv, member * row_local, row_local, 1)
    keys = mine[:, :, head_size : 2 * head_size].astype(jnp.float32)
    values = jnp.swapaxes(mine[:, :, 2 * head_size :].astype(jnp.float32), 0, 1)
    logit = jnp.sum(keys * gate_weight[:, None, :], axis=-1) / math.sqrt(head_size)
    decay = jax.nn.sigmoid(logit + gate_bias[:, None]).T
    unit = keys * lax.rsqrt(jnp.sum(keys * keys, axis=-1, keepdims=True) + 1e-06)
    state_now = update(
        cuts, kind, index, decay, states, got_one, (piece_a, piece_b, piece_c),
        jnp.transpose(unit, (1, 2, 0)), values
    )
    return (layer_out[None], state_now)


def from_partner(block, axis, stride):
    count = lax.axis_size(axis)
    route = []
    for low in range(count):
        high = low | 1 << stride
        if high != low and high < count:
            route += [(low, high), (high, low)]
    return lax.ppermute(block, axis, route)


def outgoing(state_now, parent_list, member, row_local, partner):
    target = jnp.bitwise_xor(member, partner)
    children = lax.dynamic_slice_in_dim(parent_list, target * row_local, row_local, 0)
    needed = children // row_local == member
    rank_index = jnp.cumsum(needed.astype(jnp.int32)) - 1
    slot_ids = jnp.arange(CAP, dtype=jnp.int32)
    chosen = jnp.sum(
        jnp.where(
            needed[None, :] & (rank_index[None, :] == slot_ids[:, None]),
            (children % row_local)[None, :],
            0,
        ),
        axis=1,
    )
    return jnp.take(state_now, chosen, axis=0)


def route(state_now, parent_list, member, row_local):
    first_out = outgoing(state_now, parent_list, member, row_local, 1)
    second_out = outgoing(state_now, parent_list, member, row_local, 2)
    corner_out = outgoing(state_now, parent_list, member, row_local, 3)
    got_one = from_partner(first_out, "rows", 0)
    got_two = from_partner(second_out, "rows", 1)
    relayed = from_partner(corner_out, "rows", 0)
    got_three = from_partner(relayed, "rows", 1)
    own_list = lax.dynamic_slice_in_dim(parent_list, member * row_local, row_local, 0)
    source = own_list // row_local
    partner = jnp.bitwise_xor(source, member)
    slot_index = jnp.arange(row_local, dtype=jnp.int32)
    earlier = (source[:, None] == source[None, :]) & (slot_index[:, None] > slot_index[None, :])
    rank_index = jnp.sum(earlier.astype(jnp.int32), axis=1)
    position = jnp.where(
        partner == 0, own_list % row_local, row_local + (partner - 1) * CAP + rank_index
    )
    pooled = jnp.concatenate([state_now, got_one, got_two, got_three], 0)
    return jnp.take(pooled, position, axis=0)


def per_device(
    token_ids,
    parents,
    states,
    embed_table,
    qkv_weight,
    gate_weight,
    gate_bias,
    norm_gain,
    out_weight,
):
    row_local = states.shape[0]
    heads = states.shape[1]
    head_size = states.shape[2]
    count = lax.axis_size("rows")
    if (
        embed_table.shape[1] == head_size
        and head_size % 128 == 0
        and count == heads
        and parents.shape[0] == 1
        and parents.shape[2] == 4 * row_local
        and parents.shape[1] * 4 == count
        and parents.shape[2] % 16 == 0
    ):
        return fast(
            token_ids, parents, states, embed_table, qkv_weight, gate_weight, gate_bias,
            norm_gain, out_weight
        )
    width = heads * head_size
    column_local = embed_table.shape[1]
    row_total = token_ids.shape[1]
    device = lax.axis_index("rows")
    member = device % 4
    user_index = device // 4
    weight_flat = qkv_weight.reshape(qkv_weight.shape[0], 3 * column_local)
    local_columns = jnp.take(embed_table, token_ids, axis=0)
    every_proj = jnp.einsum(
        "...rc,cf->...rf",
        lax.all_gather(local_columns, "rows", axis=2, tiled=True),
        weight_flat,
        preferred_element_type=jnp.float32,
    )
    state_now = states
    step_proj = every_proj[0]
    projected = step_proj.astype(jnp.bfloat16).reshape(row_total, 3, column_local)
    mine = lax.all_to_all(projected, "rows", split_axis=0, concat_axis=2, tiled=True)
    queries = mine[:, 0].reshape(row_local, heads, head_size)
    key_float = mine[:, 1].reshape(row_local, heads, head_size).astype(jnp.float32)
    values = mine[:, 2].reshape(row_local, heads, head_size).astype(jnp.float32)
    gate_logit = jnp.sum(key_float * gate_weight, axis=-1) / math.sqrt(head_size) + gate_bias
    decay_rate = jax.nn.sigmoid(gate_logit)
    key_unit = key_float * lax.rsqrt(jnp.sum(key_float * key_float, axis=-1, keepdims=True) + 1e-06)
    parent_list = lax.dynamic_index_in_dim(parents[0], user_index, 0, keepdims=False)
    prior_state = route(state_now, parent_list, member, row_local)
    new_state = (
        decay_rate[:, :, None, None] * prior_state.astype(jnp.float32)
        + key_unit[:, :, :, None] * values[:, :, None, :]
    )
    state_now = new_state.astype(jnp.bfloat16)
    readout = jnp.einsum("rhd,rhde->rhe", queries, state_now, preferred_element_type=jnp.float32)
    scaled = readout * lax.rsqrt(jnp.mean(readout * readout, axis=-1, keepdims=True) + 1e-05)
    normed = (scaled.reshape(row_local, width) * norm_gain).astype(jnp.bfloat16)
    attention = jnp.dot(
        lax.all_gather(normed, "rows", axis=0, tiled=True),
        out_weight,
        preferred_element_type=jnp.float32,
    )
    outputs = [(local_columns[0].astype(jnp.float32) + attention).astype(jnp.bfloat16)]
    return (jnp.stack(outputs), state_now)


def solution(mesh):
    placed = (
        P(None, "groups"),
        P(None, "groups", None),
        P(("groups", "rows"), None, None, None),
        P(None, "rows"),
        P(None, None, "rows"),
        P(),
        P(),
        P(),
        P(None, "rows"),
    )
    return jax.shard_map(
        per_device,
        mesh=mesh,
        in_specs=placed,
        out_specs=(P(None, "groups", "rows"), P(("groups", "rows"), None, None, None)),
        check_vma=False,
    )
```

```python
import functools
import math

import jax
import jax.numpy as jnp
from jax import lax
from jax.experimental import pallas as pl
from jax.experimental.pallas import tpu as pltpu
from jax.sharding import PartitionSpec as P

CAP = 2
AHEAD, BEHIND, MIDDLE = 2, 3, 4
ANY = pl.BlockSpec(memory_space=pl.ANY)
VM = pl.BlockSpec(memory_space=pltpu.VMEM)
SM = pl.BlockSpec(memory_space=pltpu.SMEM)


def gather_kernel(
    middle, list_ref, tok_ref, state_ref, table_ref, one_ref, far_ref, two_ref, three_ref, out_ref,
    buf, rows_in, wide, rows_out, in_sem, out_sem, row_sem, mid_sem
):
    device = lax.axis_index("rows")
    member, user = device % 4, device // 4
    row_local = state_ref.shape[0]
    loads = []
    for slot in list(range(CAP, 3 * CAP)) + list(range(CAP)):
        partner, order = slot // CAP + 1, slot % CAP
        base = jnp.bitwise_xor(member, partner) * row_local
        seen, chosen = jnp.int32(0), jnp.int32(0)
        for child in range(row_local):
            parent = list_ref[0, user, base + child]
            needed = parent // row_local == member
            chosen = jnp.where(needed & (seen == order), parent % row_local, chosen)
            seen = seen + needed.astype(jnp.int32)
        load = pltpu.make_async_copy(state_ref.at[chosen], buf.at[slot], in_sem.at[slot])
        load.start()
        loads.append((slot, load))
    count = out_ref.shape[0]

    def begin(i, carry):
        pltpu.make_async_copy(table_ref.at[tok_ref[0, i] // 8], rows_in.at[i], row_sem).start()
        return carry

    lax.fori_loop(0, count, begin, 0, unroll=8)
    stores = []
    for slot, load in loads:
        load.wait()
        target = one_ref.at[slot] if slot < CAP else far_ref.at[slot - CAP]
        store = pltpu.make_async_copy(buf.at[slot], target, out_sem.at[slot])
        store.start()
        stores.append(store)
        if slot >= CAP:
            half = (two_ref, three_ref)[slot // CAP - 1]
            store = pltpu.make_async_copy(
                buf.at[slot, pl.ds(*middle)], half.at[slot % CAP], mid_sem.at[slot - CAP]
            )
            store.start()
            stores.append(store)
    pltpu.make_async_copy(table_ref.at[pl.ds(0, count)], rows_in, row_sem).wait()
    wide[...] = rows_in[...].astype(jnp.float32).reshape(wide.shape)

    def pick(i, carry):
        rows_out[pl.ds(i, 1), :] = wide[pl.ds(i * 8 + tok_ref[0, i] % 8, 1), :]
        return carry

    lax.fori_loop(0, count, pick, 0, unroll=8)
    out_ref[...] = rows_out[...].astype(jnp.bfloat16)
    for store in stores:
        store.wait()


def gather(middle, parents, tokens, states, table):
    rest = states.shape[1:]
    slots = 3 * CAP
    count, width = tokens.shape[1], table.shape[1]
    size = slots * math.prod(rest) * 2
    return pl.pallas_call(
        functools.partial(gather_kernel, middle),
        out_shape=(
            jax.ShapeDtypeStruct((CAP,) + rest, states.dtype),
            jax.ShapeDtypeStruct((2 * CAP,) + rest, states.dtype),
            jax.ShapeDtypeStruct((CAP, middle[1]) + rest[1:], states.dtype),
            jax.ShapeDtypeStruct((CAP, middle[1]) + rest[1:], states.dtype),
            jax.ShapeDtypeStruct((count, width), table.dtype),
        ),
        in_specs=[SM, SM, ANY, ANY],
        out_specs=(ANY, ANY, ANY, ANY, VM),
        scratch_shapes=[
            pltpu.VMEM((slots,) + rest, states.dtype),
            pltpu.VMEM((count, 8, width), table.dtype),
            pltpu.VMEM((count * 8, width), jnp.float32),
            pltpu.VMEM((count, width), jnp.float32),
            pltpu.SemaphoreType.DMA((slots,)),
            pltpu.SemaphoreType.DMA((slots,)),
            pltpu.SemaphoreType.DMA,
            pltpu.SemaphoreType.DMA((2 * CAP,)),
        ],
        cost_estimate=pl.CostEstimate(flops=0, bytes_accessed=2 * size, transcendentals=0),
        name="gather_rows",
    )(parents, tokens, states, table.reshape(table.shape[0] // 8, 8, width))


def greet(peers):
    barrier = pltpu.get_barrier_semaphore()
    for peer in peers:
        pl.semaphore_signal(
            barrier, inc=1, device_id={"rows": peer}, device_id_type=pl.DeviceIdType.MESH
        )
    pl.semaphore_wait(barrier, len(peers))


def remote(source, target_ref, out_sem, in_sem, target):
    return pltpu.make_async_remote_copy(
        src_ref=source,
        dst_ref=target_ref,
        send_sem=out_sem,
        recv_sem=in_sem,
        device_id={"rows": target},
        device_id_type=pl.DeviceIdType.MESH,
    )


def neighbours(count):
    me = lax.axis_index("rows")
    member, my_level = me % 4, me // 4
    side_member = (member + 2) % 4
    twin_member = member + 1 - 2 * (member % 2)
    diag_member = (twin_member + 2) % 4
    levels = [(my_level + k) % (count // 4) for k in range(1, count // 4)]
    return me, my_level, member, side_member, twin_member, diag_member, levels


def phase(count, spans, mode, in_ref, out_ref, stage, sems, bulk):
    send_sem, recv_sem, own_sem = sems
    me, my_level, member, side_member, twin_member, diag_member, levels = neighbours(count)
    side, twin, diag = (my_level * 4 + m for m in (side_member, twin_member, diag_member))
    peers = [other * 4 + member for other in levels]
    side_peers = [other * 4 + side_member for other in levels]

    def place(block):
        if mode == "columns":
            return out_ref.at[:, pl.ds(pl.multiple_of(block * spans, spans), spans)]
        return out_ref.at[pl.ds(pl.multiple_of(block * spans, spans), spans)]

    def part(ref, other):
        if mode == "exchange":
            return ref.at[pl.ds(pl.multiple_of(other * spans, spans), spans)]
        return ref

    sent = []

    def send(source, block, target, target_ref=None):
        target_ref = place(block) if target_ref is None else target_ref
        copy = remote(source, target_ref, send_sem.at[len(sent)], recv_sem.at[block], target)
        copy.start()
        sent.append(copy)

    def arrived(block, ref=None):
        ref = place(block) if ref is None else ref
        remote(ref, ref, send_sem.at[0], recv_sem.at[block], twin).wait_recv()

    landing = stage if mode == "exchange" else place(side)
    send(in_ref, me, side, stage if mode == "exchange" else None)
    for other in levels:
        send(part(in_ref, other), me, other * 4 + member)
    send(part(in_ref, my_level), me, twin)
    for copy in bulk:
        copy.start()
    own = pltpu.make_async_copy(part(in_ref, my_level), place(me), own_sem.at[0])
    own.start()
    arrived(side, landing)
    for other in levels:
        send(part(landing, other), side, other * 4 + member)
    send(part(landing, my_level), side, twin)
    if mode == "exchange":
        extra = pltpu.make_async_copy(part(stage, my_level), place(side), own_sem.at[1])
        extra.start()
    for peer in peers + side_peers:
        arrived(peer)
        send(place(peer), peer, twin)
    arrived(twin)
    arrived(diag)
    for other in levels:
        arrived(other * 4 + twin_member)
        arrived(other * 4 + diag_member)
    own.wait()
    if mode == "exchange":
        extra.wait()
    return sent


def far_copies(count, far_ref, got_ref, first, offset, heads, out_sem, in_sem, at):
    _, my_level, _, side_member, _, diag_member, _ = neighbours(count)
    return [
        remote(
            far_ref.at[slot, pl.ds(first + offset, heads)],
            got_ref.at[slot, pl.ds(offset, heads)],
            out_sem.at[at + slot],
            in_sem.at[at + slot],
            my_level * 4 + (side_member if slot < CAP else diag_member),
        )
        for slot in range(2 * CAP)
    ]


def meet(count):
    _, my_level, member, side_member, twin_member, diag_member, levels = neighbours(count)
    greet(
        [my_level * 4 + m for m in (side_member, twin_member, diag_member)]
        + [other * 4 + member for other in levels]
    )


def inputs_kernel(
    count, beams, split, in_ref, weight_ref, far_ref, one_ref, out_ref, got_ref, got_one_ref,
    weights, every, proj, stage, weight_sem, send_a, recv_a, own_a, send_b, recv_b, own_b,
    bulk_send, bulk_recv
):
    column_local = in_ref.shape[1]
    load = pltpu.make_async_copy(weight_ref, weights, weight_sem)
    load.start()
    meet(count)
    _, my_level, _, _, twin_member, _, _ = neighbours(count)
    ahead = far_copies(count, far_ref, got_ref, 0, 0, split[0], bulk_send, bulk_recv, 0)
    behind = far_copies(
        count, far_ref, got_ref, 0, split[0], split[1], bulk_send, bulk_recv, 2 * CAP
    )
    behind.append(
        remote(
            one_ref, got_one_ref, bulk_send.at[4 * CAP], bulk_recv.at[4 * CAP],
            my_level * 4 + twin_member,
        )
    )
    sent = phase(
        count, column_local, "columns", in_ref, every, None, (send_a, recv_a, own_a), ahead
    )
    load.wait()
    for slab in range(3):
        proj[:, slab * column_local : (slab + 1) * column_local] = jnp.dot(
            every[...], weights[slab], preferred_element_type=jnp.float32
        ).astype(jnp.bfloat16)
    sent += phase(count, beams, "exchange", proj, out_ref, stage, (send_b, recv_b, own_b), behind)
    for copy in sent:
        copy.wait_send()
    for copy in ahead + behind:
        copy.wait()


def inputs(local_columns, weights, far, one, count, beams, split):
    row_total, column_local = local_columns.shape
    depth = weights.shape[1]
    sems = [
        pltpu.SemaphoreType.DMA((count - 1,)),
        pltpu.SemaphoreType.DMA((count,)),
        pltpu.SemaphoreType.DMA((2,)),
    ]
    return pl.pallas_call(
        functools.partial(inputs_kernel, count, beams, split),
        out_shape=(
            jax.ShapeDtypeStruct((count * beams, 3 * column_local), jnp.bfloat16),
            jax.ShapeDtypeStruct((far.shape[0], sum(split)) + far.shape[2:], far.dtype),
            jax.ShapeDtypeStruct(one.shape, one.dtype),
        ),
        in_specs=[VM, ANY, ANY, ANY],
        out_specs=(VM, ANY, ANY),
        scratch_shapes=[
            pltpu.VMEM(weights.shape, weights.dtype),
            pltpu.VMEM((row_total, depth), jnp.bfloat16),
            pltpu.VMEM((row_total, 3 * column_local), jnp.bfloat16),
            pltpu.VMEM((row_total, 3 * column_local), jnp.bfloat16),
            pltpu.SemaphoreType.DMA,
        ]
        + sems
        + sems
        + [pltpu.SemaphoreType.DMA((4 * CAP + 1,)), pltpu.SemaphoreType.DMA((4 * CAP + 1,))],
        compiler_params=pltpu.CompilerParams(collective_id=1, has_side_effects=True),
        name="spread_inputs",
    )(local_columns, weights, far, one)


def normed_kernel(
    count, first, heads, in_ref, far_ref, out_ref, got_ref, send_a, recv_a, own_a, bulk_send,
    bulk_recv
):
    meet(count)
    bulk = far_copies(count, far_ref, got_ref, first, 0, heads, bulk_send, bulk_recv, 0)
    sent = phase(
        count, in_ref.shape[0], "rows", in_ref, out_ref, None, (send_a, recv_a, own_a), bulk
    )
    for copy in sent:
        copy.wait_send()
    for copy in bulk:
        copy.wait()


def spread_normed(normed, far, count, first, heads):
    return pl.pallas_call(
        functools.partial(normed_kernel, count, first, heads),
        out_shape=(
            jax.ShapeDtypeStruct((count * normed.shape[0], normed.shape[1]), normed.dtype),
            jax.ShapeDtypeStruct((far.shape[0], heads) + far.shape[2:], far.dtype),
        ),
        in_specs=[VM, ANY],
        out_specs=(VM, ANY),
        scratch_shapes=[
            pltpu.SemaphoreType.DMA((count - 1,)),
            pltpu.SemaphoreType.DMA((count,)),
            pltpu.SemaphoreType.DMA((2,)),
            pltpu.SemaphoreType.DMA((2 * CAP,)),
            pltpu.SemaphoreType.DMA((2 * CAP,)),
        ],
        compiler_params=pltpu.CompilerParams(collective_id=2, has_side_effects=True),
        name="spread_normed",
    )(normed, far)


def read_kernel(
    head_size, bias_ref, qkv_ref, state_ref, weight_ref, gain_ref, owner_ref, slot_ref, out_ref
):
    step = pl.program_id(0)
    group = qkv_ref.shape[0]
    masks = [owner_ref[:, p : p + 1] > 0 for p in range(state_ref.shape[0])]
    for head in range(group):
        block = qkv_ref[head]
        q_half = block[:, :head_size]
        queries = q_half.astype(jnp.float32)
        keys = block[:, head_size : 2 * head_size].astype(jnp.float32)
        values = block[:, 2 * head_size :].astype(jnp.float32)
        logit = jnp.sum(keys * weight_ref[head], axis=-1, keepdims=True) / math.sqrt(head_size)
        decay = jax.nn.sigmoid(logit + bias_ref[step * group + head])
        unit = keys * lax.rsqrt(jnp.sum(keys * keys, axis=-1, keepdims=True) + 1e-06)
        spreadq = jnp.concatenate(
            [jnp.where(mask, queries, 0.0).astype(jnp.bfloat16) for mask in masks], axis=1
        )
        stacked = state_ref[:, head].reshape(state_ref.shape[0] * head_size, head_size)
        total = jnp.dot(spreadq, stacked, preferred_element_type=jnp.float32)
        readout = decay * total + jnp.sum(queries * unit, axis=-1, keepdims=True) * values
        scaled = readout * lax.rsqrt(jnp.mean(readout * readout, axis=-1, keepdims=True) + 1e-05)
        normed = (scaled * gain_ref[head]).astype(jnp.bfloat16)
        picked = jnp.dot(slot_ref[...], normed, preferred_element_type=jnp.float32)
        out_ref[:, head * head_size : (head + 1) * head_size] = picked.astype(jnp.bfloat16)


def read(qkv, states, gate_weight, gate_bias, norm_gain, owner, slot_pick):
    heads, beams, triple = qkv.shape
    row_local, _, head_size, _ = states.shape
    slots = slot_pick.shape[0]
    group = 4 if heads % 4 == 0 else 1
    return pl.pallas_call(
        functools.partial(read_kernel, head_size),
        grid=(heads // group,),
        out_shape=jax.ShapeDtypeStruct((slots, heads * head_size), jnp.bfloat16),
        in_specs=[
            SM,
            pl.BlockSpec((group, beams, triple), lambda h: (h, 0, 0)),
            pl.BlockSpec((row_local, group, head_size, head_size), lambda h: (0, h, 0, 0)),
            pl.BlockSpec((group, 1, head_size), lambda h: (h, 0, 0)),
            pl.BlockSpec((group, 1, head_size), lambda h: (h, 0, 0)),
            pl.BlockSpec((beams, row_local), lambda h: (0, 0)),
            pl.BlockSpec((slots, beams), lambda h: (0, 0)),
        ],
        out_specs=pl.BlockSpec((slots, group * head_size), lambda h: (0, h)),
        cost_estimate=pl.CostEstimate(
            flops=2 * beams * math.prod(states.shape),
            bytes_accessed=2 * math.prod(states.shape),
            transcendentals=0,
        ),
        name="read_heads",
    )(
        gate_bias,
        qkv,
        states,
        gate_weight.reshape(heads, 1, head_size),
        norm_gain.reshape(heads, 1, head_size),
        owner,
        slot_pick,
    )


def update_kernel(
    cuts, kind_ref, index_ref, decay_ref, state_ref, one_ref, two_ref, three_ref, early_ref,
    late_ref, unit_ref, value_ref, out_ref, old, new, in_sem, out_sem
):
    row_local, heads = old.shape[0], old.shape[1]
    for row in range(row_local):
        @pl.when(kind_ref[row] == 0)
        def _():
            pltpu.make_async_copy(
                state_ref.at[index_ref[row]], old.at[row], in_sem.at[row]
            ).start()

        @pl.when(kind_ref[row] == 1)
        def _():
            pltpu.make_async_copy(one_ref.at[index_ref[row]], old.at[row], in_sem.at[row]).start()

        @pl.when(kind_ref[row] > 1)
        def _():
            slot = (kind_ref[row] - 2) * CAP + index_ref[row]
            for cut, piece in ((cuts[0], early_ref), (cuts[2], late_ref)):
                pltpu.make_async_copy(
                    piece.at[slot], old.at[row, pl.ds(*cut)], in_sem.at[row]
                ).start()

        for other, piece in ((2, two_ref), (3, three_ref)):
            @pl.when(kind_ref[row] == other)
            def _():
                pltpu.make_async_copy(
                    piece.at[index_ref[row]], old.at[row, pl.ds(*cuts[1])], in_sem.at[row]
                ).start()

    def step(row, carry):
        pltpu.make_async_copy(state_ref.at[0], old.at[row], in_sem.at[row]).wait()
        columns = unit_ref[row]
        values = value_ref[row]
        for head in range(heads):
            fresh = columns[:, head : head + 1] * values[head : head + 1, :]
            prior = old[row, head].astype(jnp.float32)
            new[row, head] = (decay_ref[row, head] * prior + fresh).astype(jnp.bfloat16)
        pltpu.make_async_copy(new.at[row], out_ref.at[row], out_sem.at[row]).start()
        return carry

    lax.fori_loop(0, row_local, step, 0)
    for row in range(row_local):
        pltpu.make_async_copy(new.at[row], out_ref.at[row], out_sem.at[row]).wait()


def update(cuts, kind, index, decay, states, pieces, unit, values):
    row_local = states.shape[0]
    return pl.pallas_call(
        functools.partial(update_kernel, cuts),
        out_shape=jax.ShapeDtypeStruct(states.shape, states.dtype),
        in_specs=[SM, SM, SM, ANY] + [ANY] * len(pieces) + [VM, VM],
        out_specs=ANY,
        scratch_shapes=[
            pltpu.VMEM(states.shape, states.dtype),
            pltpu.VMEM(states.shape, states.dtype),
            pltpu.SemaphoreType.DMA((row_local,)),
            pltpu.SemaphoreType.DMA((row_local,)),
        ],
        cost_estimate=pl.CostEstimate(
            flops=4 * math.prod(states.shape),
            bytes_accessed=4 * math.prod(states.shape),
            transcendentals=0,
        ),
        name="update_states",
    )(kind, index, decay, states, *pieces, unit, values)


def swap(block, partner):
    count = lax.axis_size("rows")
    return lax.ppermute(block, "rows", [(low, low ^ partner) for low in range(count)])


def fast(
    token_ids, parents, states, embed_table, qkv_weight, gate_weight, gate_bias, norm_gain,
    out_weight
):
    row_local, heads, head_size, _ = states.shape
    column_local = embed_table.shape[1]
    row_total = token_ids.shape[1]
    users, beams = parents.shape[1], parents.shape[2]
    count = lax.axis_size("rows")
    device = lax.axis_index("rows")
    member, user = device % 4, device // 4
    slots = 16 * ((row_local + 3 * CAP + 15) // 16)

    split = (heads * AHEAD // 16, heads * BEHIND // 16)
    middle = heads * MIDDLE // 16
    early = sum(split)
    cuts = ((0, early), (early, middle), (early + middle, heads - early - middle))
    one, far, two, three, local_columns = gather(
        cuts[1], parents, token_ids, states, embed_table
    )
    qkv, piece_a, got_one = inputs(
        local_columns, jnp.transpose(qkv_weight, (1, 0, 2)), far, one, count, beams, split
    )
    two, three, qkv, lists = lax.optimization_barrier((two, three, qkv, parents[0]))
    got_two = swap(two, 2)
    got_three = swap(three, 3)
    qkv = qkv.reshape(count, beams, 3 * column_local)

    owner_block = lists // row_local
    blocks = owner_block.reshape(users, 4, row_local)
    at = jnp.arange(row_local, dtype=jnp.int32)
    same = (blocks[..., :, None] == blocks[..., None, :]) & (at[:, None] > at[None, :])
    rank = jnp.sum(same.astype(jnp.int32), axis=-1)
    offset = jnp.bitwise_xor(blocks, jnp.arange(4, dtype=jnp.int32)[None, :, None])
    slot = jnp.where(offset == 0, at[None, None, :], row_local + (offset - 1) * CAP + rank)
    slot = slot.reshape(users, beams)
    my_list = lax.dynamic_index_in_dim(lists, user, 0, keepdims=False)
    my_slot = lax.dynamic_index_in_dim(slot, user, 0, keepdims=False)
    held = my_list // row_local == member
    within = my_list % row_local
    slot_pick = held[None, :] & (my_slot[None, :] == jnp.arange(slots, dtype=jnp.int32)[:, None])
    owner = (held[:, None] & (within[:, None] == at[None, :])).astype(jnp.float32)
    own_slot = lax.dynamic_slice_in_dim(my_slot, member * row_local, row_local, 0)
    own_within = lax.dynamic_slice_in_dim(within, member * row_local, row_local, 0)
    far_row = own_slot >= row_local
    kind = jnp.where(far_row, (own_slot - row_local) // CAP + 1, 0)
    index = jnp.where(far_row, (own_slot - row_local) % CAP, own_within)
    source = (
        (jnp.arange(users, dtype=jnp.int32)[:, None] * 4 + owner_block) * slots + slot
    ).reshape(row_total)
    pick = (source[:, None] == jnp.arange(count * slots, dtype=jnp.int32)[None, :]).astype(
        jnp.bfloat16
    )

    normed = read(
        qkv, states, gate_weight, gate_bias, norm_gain, owner, slot_pick.astype(jnp.bfloat16)
    )
    mine = lax.dynamic_slice_in_dim(qkv, member * row_local, row_local, 1)
    keys = mine[:, :, head_size : 2 * head_size].astype(jnp.float32)
    values = jnp.swapaxes(mine[:, :, 2 * head_size :].astype(jnp.float32), 0, 1)
    logit = jnp.sum(keys * gate_weight[:, None, :], axis=-1) / math.sqrt(head_size)
    decay = jax.nn.sigmoid(logit + gate_bias[:, None]).T
    unit = keys * lax.rsqrt(jnp.sum(keys * keys, axis=-1, keepdims=True) + 1e-06)
    unit = jnp.transpose(unit, (1, 2, 0))
    normed, pick, decay, unit, values, kind, index = lax.optimization_barrier(
        (normed, pick, decay, unit, values, kind, index)
    )
    every_normed, piece_c = spread_normed(normed, far, count, *cuts[2])
    ordered = jnp.dot(pick, every_normed, preferred_element_type=jnp.float32)
    attention = jnp.dot(
        ordered.astype(jnp.bfloat16), out_weight, preferred_element_type=jnp.float32
    )
    layer_out = (local_columns.astype(jnp.float32) + attention).astype(jnp.bfloat16)
    state_now = update(
        cuts, kind, index, decay, states,
        (got_one, got_two, got_three, piece_a, piece_c), unit, values
    )
    return (layer_out[None], state_now)


def from_partner(block, axis, stride):
    count = lax.axis_size(axis)
    route = []
    for low in range(count):
        high = low | 1 << stride
        if high != low and high < count:
            route += [(low, high), (high, low)]
    return lax.ppermute(block, axis, route)


def outgoing(state_now, parent_list, member, row_local, partner):
    target = jnp.bitwise_xor(member, partner)
    children = lax.dynamic_slice_in_dim(parent_list, target * row_local, row_local, 0)
    needed = children // row_local == member
    rank_index = jnp.cumsum(needed.astype(jnp.int32)) - 1
    slot_ids = jnp.arange(CAP, dtype=jnp.int32)
    chosen = jnp.sum(
        jnp.where(
            needed[None, :] & (rank_index[None, :] == slot_ids[:, None]),
            (children % row_local)[None, :],
            0,
        ),
        axis=1,
    )
    return jnp.take(state_now, chosen, axis=0)


def route(state_now, parent_list, member, row_local):
    first_out = outgoing(state_now, parent_list, member, row_local, 1)
    second_out = outgoing(state_now, parent_list, member, row_local, 2)
    corner_out = outgoing(state_now, parent_list, member, row_local, 3)
    got_one = from_partner(first_out, "rows", 0)
    got_two = from_partner(second_out, "rows", 1)
    relayed = from_partner(corner_out, "rows", 0)
    got_three = from_partner(relayed, "rows", 1)
    own_list = lax.dynamic_slice_in_dim(parent_list, member * row_local, row_local, 0)
    source = own_list // row_local
    partner = jnp.bitwise_xor(source, member)
    slot_index = jnp.arange(row_local, dtype=jnp.int32)
    earlier = (source[:, None] == source[None, :]) & (slot_index[:, None] > slot_index[None, :])
    rank_index = jnp.sum(earlier.astype(jnp.int32), axis=1)
    position = jnp.where(
        partner == 0, own_list % row_local, row_local + (partner - 1) * CAP + rank_index
    )
    pooled = jnp.concatenate([state_now, got_one, got_two, got_three], 0)
    return jnp.take(pooled, position, axis=0)


def per_device(
    token_ids,
    parents,
    states,
    embed_table,
    qkv_weight,
    gate_weight,
    gate_bias,
    norm_gain,
    out_weight,
):
    row_local = states.shape[0]
    heads = states.shape[1]
    head_size = states.shape[2]
    count = lax.axis_size("rows")
    if (
        embed_table.shape[1] == head_size
        and head_size % 128 == 0
        and count == heads
        and parents.shape[0] == 1
        and parents.shape[2] == 4 * row_local
        and parents.shape[1] * 4 == count
        and parents.shape[2] % 16 == 0
    ):
        return fast(
            token_ids, parents, states, embed_table, qkv_weight, gate_weight, gate_bias,
            norm_gain, out_weight
        )
    width = heads * head_size
    column_local = embed_table.shape[1]
    row_total = token_ids.shape[1]
    device = lax.axis_index("rows")
    member = device % 4
    user_index = device // 4
    weight_flat = qkv_weight.reshape(qkv_weight.shape[0], 3 * column_local)
    local_columns = jnp.take(embed_table, token_ids, axis=0)
    every_proj = jnp.einsum(
        "...rc,cf->...rf",
        lax.all_gather(local_columns, "rows", axis=2, tiled=True),
        weight_flat,
        preferred_element_type=jnp.float32,
    )
    state_now = states
    step_proj = every_proj[0]
    projected = step_proj.astype(jnp.bfloat16).reshape(row_total, 3, column_local)
    mine = lax.all_to_all(projected, "rows", split_axis=0, concat_axis=2, tiled=True)
    queries = mine[:, 0].reshape(row_local, heads, head_size)
    key_float = mine[:, 1].reshape(row_local, heads, head_size).astype(jnp.float32)
    values = mine[:, 2].reshape(row_local, heads, head_size).astype(jnp.float32)
    gate_logit = jnp.sum(key_float * gate_weight, axis=-1) / math.sqrt(head_size) + gate_bias
    decay_rate = jax.nn.sigmoid(gate_logit)
    key_unit = key_float * lax.rsqrt(jnp.sum(key_float * key_float, axis=-1, keepdims=True) + 1e-06)
    parent_list = lax.dynamic_index_in_dim(parents[0], user_index, 0, keepdims=False)
    prior_state = route(state_now, parent_list, member, row_local)
    new_state = (
        decay_rate[:, :, None, None] * prior_state.astype(jnp.float32)
        + key_unit[:, :, :, None] * values[:, :, None, :]
    )
    state_now = new_state.astype(jnp.bfloat16)
    readout = jnp.einsum("rhd,rhde->rhe", queries, state_now, preferred_element_type=jnp.float32)
    scaled = readout * lax.rsqrt(jnp.mean(readout * readout, axis=-1, keepdims=True) + 1e-05)
    normed = (scaled.reshape(row_local, width) * norm_gain).astype(jnp.bfloat16)
    attention = jnp.dot(
        lax.all_gather(normed, "rows", axis=0, tiled=True),
        out_weight,
        preferred_element_type=jnp.float32,
    )
    outputs = [(local_columns[0].astype(jnp.float32) + attention).astype(jnp.bfloat16)]
    return (jnp.stack(outputs), state_now)


def solution(mesh):
    placed = (
        P(None, "groups"),
        P(None, "groups", None),
        P(("groups", "rows"), None, None, None),
        P(None, "rows"),
        P(None, None, "rows"),
        P(),
        P(),
        P(),
        P(None, "rows"),
    )
    return jax.shard_map(
        per_device,
        mesh=mesh,
        in_specs=placed,
        out_specs=(P(None, "groups", "rows"), P(("groups", "rows"), None, None, None)),
        check_vma=False,
    )
```

```python
import functools
import math

import jax
import jax.numpy as jnp
from jax import lax
from jax.experimental import pallas as pl
from jax.experimental.pallas import tpu as pltpu
from jax.sharding import PartitionSpec as P

CAP = 2
AHEAD, BEHIND, MIDDLE = 3, 2, 7
ANY = pl.BlockSpec(memory_space=pl.ANY)
VM = pl.BlockSpec(memory_space=pltpu.VMEM)
SM = pl.BlockSpec(memory_space=pltpu.SMEM)


def gather_kernel(
    middle, list_ref, tok_ref, state_ref, table_ref, one_ref, far_ref, two_ref, three_ref, out_ref,
    buf, rows_in, wide, rows_out, in_sem, out_sem, row_sem, mid_sem
):
    device = lax.axis_index("rows")
    member, user = device % 4, device // 4
    row_local = state_ref.shape[0]
    loads = []
    for slot in list(range(CAP, 3 * CAP)) + list(range(CAP)):
        partner, order = slot // CAP + 1, slot % CAP
        base = jnp.bitwise_xor(member, partner) * row_local
        seen, chosen = jnp.int32(0), jnp.int32(0)
        for child in range(row_local):
            parent = list_ref[0, user, base + child]
            needed = parent // row_local == member
            chosen = jnp.where(needed & (seen == order), parent % row_local, chosen)
            seen = seen + needed.astype(jnp.int32)
        load = pltpu.make_async_copy(state_ref.at[chosen], buf.at[slot], in_sem.at[slot])
        load.start()
        loads.append((slot, load))
    count = out_ref.shape[0]

    def begin(i, carry):
        pltpu.make_async_copy(table_ref.at[tok_ref[0, i] // 8], rows_in.at[i], row_sem).start()
        return carry

    lax.fori_loop(0, count, begin, 0, unroll=8)
    stores = []
    for slot, load in loads:
        load.wait()
        target = one_ref.at[slot] if slot < CAP else far_ref.at[slot - CAP]
        store = pltpu.make_async_copy(buf.at[slot], target, out_sem.at[slot])
        store.start()
        stores.append(store)
        if slot >= CAP:
            half = (two_ref, three_ref)[slot // CAP - 1]
            store = pltpu.make_async_copy(
                buf.at[slot, pl.ds(*middle)], half.at[slot % CAP], mid_sem.at[slot - CAP]
            )
            store.start()
            stores.append(store)
    pltpu.make_async_copy(table_ref.at[pl.ds(0, count)], rows_in, row_sem).wait()
    wide[...] = rows_in[...].astype(jnp.float32).reshape(wide.shape)

    def pick(i, carry):
        rows_out[pl.ds(i, 1), :] = wide[pl.ds(i * 8 + tok_ref[0, i] % 8, 1), :]
        return carry

    lax.fori_loop(0, count, pick, 0, unroll=8)
    out_ref[...] = rows_out[...].astype(jnp.bfloat16)
    for store in stores:
        store.wait()


def gather(middle, parents, tokens, states, table):
    rest = states.shape[1:]
    slots = 3 * CAP
    count, width = tokens.shape[1], table.shape[1]
    size = slots * math.prod(rest) * 2
    return pl.pallas_call(
        functools.partial(gather_kernel, middle),
        out_shape=(
            jax.ShapeDtypeStruct((CAP,) + rest, states.dtype),
            jax.ShapeDtypeStruct((2 * CAP,) + rest, states.dtype),
            jax.ShapeDtypeStruct((CAP, middle[1]) + rest[1:], states.dtype),
            jax.ShapeDtypeStruct((CAP, middle[1]) + rest[1:], states.dtype),
            jax.ShapeDtypeStruct((count, width), table.dtype),
        ),
        in_specs=[SM, SM, ANY, ANY],
        out_specs=(ANY, ANY, ANY, ANY, VM),
        scratch_shapes=[
            pltpu.VMEM((slots,) + rest, states.dtype),
            pltpu.VMEM((count, 8, width), table.dtype),
            pltpu.VMEM((count * 8, width), jnp.float32),
            pltpu.VMEM((count, width), jnp.float32),
            pltpu.SemaphoreType.DMA((slots,)),
            pltpu.SemaphoreType.DMA((slots,)),
            pltpu.SemaphoreType.DMA,
            pltpu.SemaphoreType.DMA((2 * CAP,)),
        ],
        cost_estimate=pl.CostEstimate(flops=0, bytes_accessed=2 * size, transcendentals=0),
        name="gather_rows",
    )(parents, tokens, states, table.reshape(table.shape[0] // 8, 8, width))


def greet(peers):
    barrier = pltpu.get_barrier_semaphore()
    for peer in peers:
        pl.semaphore_signal(
            barrier, inc=1, device_id={"rows": peer}, device_id_type=pl.DeviceIdType.MESH
        )
    pl.semaphore_wait(barrier, len(peers))


def remote(source, target_ref, out_sem, in_sem, target):
    return pltpu.make_async_remote_copy(
        src_ref=source,
        dst_ref=target_ref,
        send_sem=out_sem,
        recv_sem=in_sem,
        device_id={"rows": target},
        device_id_type=pl.DeviceIdType.MESH,
    )


def neighbours(count):
    me = lax.axis_index("rows")
    member, my_level = me % 4, me // 4
    side_member = (member + 2) % 4
    twin_member = member + 1 - 2 * (member % 2)
    diag_member = (twin_member + 2) % 4
    levels = [(my_level + k) % (count // 4) for k in range(1, count // 4)]
    return me, my_level, member, side_member, twin_member, diag_member, levels


def phase(count, spans, mode, in_ref, out_ref, stage, sems, bulk):
    send_sem, recv_sem, own_sem = sems
    me, my_level, member, side_member, twin_member, diag_member, levels = neighbours(count)
    side, twin, diag = (my_level * 4 + m for m in (side_member, twin_member, diag_member))
    peers = [other * 4 + member for other in levels]
    side_peers = [other * 4 + side_member for other in levels]

    def place(block):
        if mode == "columns":
            return out_ref.at[:, pl.ds(pl.multiple_of(block * spans, spans), spans)]
        return out_ref.at[pl.ds(pl.multiple_of(block * spans, spans), spans)]

    def part(ref, other):
        if mode == "exchange":
            return ref.at[pl.ds(pl.multiple_of(other * spans, spans), spans)]
        return ref

    sent = []

    def send(source, block, target, target_ref=None):
        target_ref = place(block) if target_ref is None else target_ref
        copy = remote(source, target_ref, send_sem.at[len(sent)], recv_sem.at[block], target)
        copy.start()
        sent.append(copy)

    def arrived(block, ref=None):
        ref = place(block) if ref is None else ref
        remote(ref, ref, send_sem.at[0], recv_sem.at[block], twin).wait_recv()

    landing = stage if mode == "exchange" else place(side)
    send(in_ref, me, side, stage if mode == "exchange" else None)
    for other in levels:
        send(part(in_ref, other), me, other * 4 + member)
    send(part(in_ref, my_level), me, twin)
    for copy in bulk:
        copy.start()
    own = pltpu.make_async_copy(part(in_ref, my_level), place(me), own_sem.at[0])
    own.start()
    arrived(side, landing)
    for other in levels:
        send(part(landing, other), side, other * 4 + member)
    send(part(landing, my_level), side, twin)
    if mode == "exchange":
        extra = pltpu.make_async_copy(part(stage, my_level), place(side), own_sem.at[1])
        extra.start()
    for peer in peers + side_peers:
        arrived(peer)
        send(place(peer), peer, twin)
    arrived(twin)
    arrived(diag)
    for other in levels:
        arrived(other * 4 + twin_member)
        arrived(other * 4 + diag_member)
    own.wait()
    if mode == "exchange":
        extra.wait()
    return sent


def far_copies(count, far_ref, got_ref, first, offset, heads, out_sem, in_sem, at):
    _, my_level, _, side_member, _, diag_member, _ = neighbours(count)
    return [
        remote(
            far_ref.at[slot, pl.ds(first + offset, heads)],
            got_ref.at[slot, pl.ds(offset, heads)],
            out_sem.at[at + slot],
            in_sem.at[at + slot],
            my_level * 4 + (side_member if slot < CAP else diag_member),
        )
        for slot in range(2 * CAP)
    ]


def meet(count):
    _, my_level, member, side_member, twin_member, diag_member, levels = neighbours(count)
    greet(
        [my_level * 4 + m for m in (side_member, twin_member, diag_member)]
        + [other * 4 + member for other in levels]
    )


def inputs_kernel(
    count, beams, split, in_ref, weight_ref, far_ref, one_ref, out_ref, got_ref, got_one_ref,
    weights, every, proj, stage, weight_sem, send_a, recv_a, own_a, send_b, recv_b, own_b,
    bulk_send, bulk_recv
):
    column_local = in_ref.shape[1]
    load = pltpu.make_async_copy(weight_ref, weights, weight_sem)
    load.start()
    meet(count)
    _, my_level, _, _, twin_member, _, _ = neighbours(count)
    ahead = far_copies(count, far_ref, got_ref, 0, 0, split[0], bulk_send, bulk_recv, 0)
    behind = far_copies(
        count, far_ref, got_ref, 0, split[0], split[1], bulk_send, bulk_recv, 2 * CAP
    )
    behind.append(
        remote(
            one_ref, got_one_ref, bulk_send.at[4 * CAP], bulk_recv.at[4 * CAP],
            my_level * 4 + twin_member,
        )
    )
    sent = phase(
        count, column_local, "columns", in_ref, every, None, (send_a, recv_a, own_a), ahead
    )
    load.wait()
    for slab in range(3):
        proj[:, slab * column_local : (slab + 1) * column_local] = jnp.dot(
            every[...], weights[slab], preferred_element_type=jnp.float32
        ).astype(jnp.bfloat16)
    sent += phase(count, beams, "exchange", proj, out_ref, stage, (send_b, recv_b, own_b), behind)
    for copy in sent:
        copy.wait_send()
    for copy in ahead + behind:
        copy.wait()


def inputs(local_columns, weights, far, one, count, beams, split):
    row_total, column_local = local_columns.shape
    depth = weights.shape[1]
    sems = [
        pltpu.SemaphoreType.DMA((count - 1,)),
        pltpu.SemaphoreType.DMA((count,)),
        pltpu.SemaphoreType.DMA((2,)),
    ]
    return pl.pallas_call(
        functools.partial(inputs_kernel, count, beams, split),
        out_shape=(
            jax.ShapeDtypeStruct((count * beams, 3 * column_local), jnp.bfloat16),
            jax.ShapeDtypeStruct((far.shape[0], sum(split)) + far.shape[2:], far.dtype),
            jax.ShapeDtypeStruct(one.shape, one.dtype),
        ),
        in_specs=[VM, ANY, ANY, ANY],
        out_specs=(VM, ANY, ANY),
        scratch_shapes=[
            pltpu.VMEM(weights.shape, weights.dtype),
            pltpu.VMEM((row_total, depth), jnp.bfloat16),
            pltpu.VMEM((row_total, 3 * column_local), jnp.bfloat16),
            pltpu.VMEM((row_total, 3 * column_local), jnp.bfloat16),
            pltpu.SemaphoreType.DMA,
        ]
        + sems
        + sems
        + [pltpu.SemaphoreType.DMA((4 * CAP + 1,)), pltpu.SemaphoreType.DMA((4 * CAP + 1,))],
        compiler_params=pltpu.CompilerParams(collective_id=1, has_side_effects=True),
        name="spread_inputs",
    )(local_columns, weights, far, one)


def normed_kernel(
    count, first, heads, in_ref, far_ref, out_ref, got_ref, send_a, recv_a, own_a, bulk_send,
    bulk_recv
):
    meet(count)
    bulk = far_copies(count, far_ref, got_ref, first, 0, heads, bulk_send, bulk_recv, 0)
    sent = phase(
        count, in_ref.shape[0], "rows", in_ref, out_ref, None, (send_a, recv_a, own_a), bulk
    )
    for copy in sent:
        copy.wait_send()
    for copy in bulk:
        copy.wait()


def spread_normed(normed, far, count, first, heads):
    return pl.pallas_call(
        functools.partial(normed_kernel, count, first, heads),
        out_shape=(
            jax.ShapeDtypeStruct((count * normed.shape[0], normed.shape[1]), normed.dtype),
            jax.ShapeDtypeStruct((far.shape[0], heads) + far.shape[2:], far.dtype),
        ),
        in_specs=[VM, ANY],
        out_specs=(VM, ANY),
        scratch_shapes=[
            pltpu.SemaphoreType.DMA((count - 1,)),
            pltpu.SemaphoreType.DMA((count,)),
            pltpu.SemaphoreType.DMA((2,)),
            pltpu.SemaphoreType.DMA((2 * CAP,)),
            pltpu.SemaphoreType.DMA((2 * CAP,)),
        ],
        compiler_params=pltpu.CompilerParams(collective_id=2, has_side_effects=True),
        name="spread_normed",
    )(normed, far)


def read_kernel(
    head_size, bias_ref, qkv_ref, state_ref, weight_ref, gain_ref, owner_ref, slot_ref, out_ref
):
    step = pl.program_id(0)
    group = qkv_ref.shape[0]
    masks = [owner_ref[:, p : p + 1] > 0 for p in range(state_ref.shape[0])]
    for head in range(group):
        block = qkv_ref[head]
        q_half = block[:, :head_size]
        queries = q_half.astype(jnp.float32)
        keys = block[:, head_size : 2 * head_size].astype(jnp.float32)
        values = block[:, 2 * head_size :].astype(jnp.float32)
        logit = jnp.sum(keys * weight_ref[head], axis=-1, keepdims=True) / math.sqrt(head_size)
        decay = jax.nn.sigmoid(logit + bias_ref[step * group + head])
        unit = keys * lax.rsqrt(jnp.sum(keys * keys, axis=-1, keepdims=True) + 1e-06)
        spreadq = jnp.concatenate(
            [jnp.where(mask, queries, 0.0).astype(jnp.bfloat16) for mask in masks], axis=1
        )
        stacked = state_ref[:, head].reshape(state_ref.shape[0] * head_size, head_size)
        total = jnp.dot(spreadq, stacked, preferred_element_type=jnp.float32)
        readout = decay * total + jnp.sum(queries * unit, axis=-1, keepdims=True) * values
        scaled = readout * lax.rsqrt(jnp.mean(readout * readout, axis=-1, keepdims=True) + 1e-05)
        normed = (scaled * gain_ref[head]).astype(jnp.bfloat16)
        picked = jnp.dot(slot_ref[...], normed, preferred_element_type=jnp.float32)
        out_ref[:, head * head_size : (head + 1) * head_size] = picked.astype(jnp.bfloat16)


def read(qkv, states, gate_weight, gate_bias, norm_gain, owner, slot_pick):
    heads, beams, triple = qkv.shape
    row_local, _, head_size, _ = states.shape
    slots = slot_pick.shape[0]
    group = 4 if heads % 4 == 0 else 1
    return pl.pallas_call(
        functools.partial(read_kernel, head_size),
        grid=(heads // group,),
        out_shape=jax.ShapeDtypeStruct((slots, heads * head_size), jnp.bfloat16),
        in_specs=[
            SM,
            pl.BlockSpec((group, beams, triple), lambda h: (h, 0, 0)),
            pl.BlockSpec((row_local, group, head_size, head_size), lambda h: (0, h, 0, 0)),
            pl.BlockSpec((group, 1, head_size), lambda h: (h, 0, 0)),
            pl.BlockSpec((group, 1, head_size), lambda h: (h, 0, 0)),
            pl.BlockSpec((beams, row_local), lambda h: (0, 0)),
            pl.BlockSpec((slots, beams), lambda h: (0, 0)),
        ],
        out_specs=pl.BlockSpec((slots, group * head_size), lambda h: (0, h)),
        cost_estimate=pl.CostEstimate(
            flops=2 * beams * math.prod(states.shape),
            bytes_accessed=2 * math.prod(states.shape),
            transcendentals=0,
        ),
        name="read_heads",
    )(
        gate_bias,
        qkv,
        states,
        gate_weight.reshape(heads, 1, head_size),
        norm_gain.reshape(heads, 1, head_size),
        owner,
        slot_pick,
    )


def update_kernel(
    cuts, kind_ref, index_ref, decay_ref, state_ref, one_ref, two_ref, three_ref, early_ref,
    late_ref, unit_ref, value_ref, out_ref, old, new, in_sem, out_sem
):
    row_local, heads = old.shape[0], old.shape[1]
    for row in range(row_local):
        @pl.when(kind_ref[row] == 0)
        def _():
            pltpu.make_async_copy(
                state_ref.at[index_ref[row]], old.at[row], in_sem.at[row]
            ).start()

        @pl.when(kind_ref[row] == 1)
        def _():
            pltpu.make_async_copy(one_ref.at[index_ref[row]], old.at[row], in_sem.at[row]).start()

        @pl.when(kind_ref[row] > 1)
        def _():
            slot = (kind_ref[row] - 2) * CAP + index_ref[row]
            for cut, piece in ((cuts[0], early_ref), (cuts[2], late_ref)):
                pltpu.make_async_copy(
                    piece.at[slot], old.at[row, pl.ds(*cut)], in_sem.at[row]
                ).start()

        for other, piece in ((2, two_ref), (3, three_ref)):
            @pl.when(kind_ref[row] == other)
            def _():
                pltpu.make_async_copy(
                    piece.at[index_ref[row]], old.at[row, pl.ds(*cuts[1])], in_sem.at[row]
                ).start()

    def step(row, carry):
        pltpu.make_async_copy(state_ref.at[0], old.at[row], in_sem.at[row]).wait()
        columns = jnp.transpose(unit_ref[row])
        values = value_ref[row]
        for head in range(heads):
            fresh = columns[:, head : head + 1] * values[head : head + 1, :]
            prior = old[row, head].astype(jnp.float32)
            new[row, head] = (decay_ref[row, head] * prior + fresh).astype(jnp.bfloat16)
        pltpu.make_async_copy(new.at[row], out_ref.at[row], out_sem.at[row]).start()
        return carry

    lax.fori_loop(0, row_local, step, 0)
    for row in range(row_local):
        pltpu.make_async_copy(new.at[row], out_ref.at[row], out_sem.at[row]).wait()


def update(cuts, kind, index, decay, states, pieces, unit, values):
    row_local = states.shape[0]
    return pl.pallas_call(
        functools.partial(update_kernel, cuts),
        out_shape=jax.ShapeDtypeStruct(states.shape, states.dtype),
        in_specs=[SM, SM, SM, ANY] + [ANY] * len(pieces) + [VM, VM],
        out_specs=ANY,
        scratch_shapes=[
            pltpu.VMEM(states.shape, states.dtype),
            pltpu.VMEM(states.shape, states.dtype),
            pltpu.SemaphoreType.DMA((row_local,)),
            pltpu.SemaphoreType.DMA((row_local,)),
        ],
        cost_estimate=pl.CostEstimate(
            flops=4 * math.prod(states.shape),
            bytes_accessed=4 * math.prod(states.shape),
            transcendentals=0,
        ),
        name="update_states",
    )(kind, index, decay, states, *pieces, unit, values)


def swap(block, partner):
    count = lax.axis_size("rows")
    return lax.ppermute(block, "rows", [(low, low ^ partner) for low in range(count)])


def fast(
    token_ids, parents, states, embed_table, qkv_weight, gate_weight, gate_bias, norm_gain,
    out_weight
):
    row_local, heads, head_size, _ = states.shape
    column_local = embed_table.shape[1]
    row_total = token_ids.shape[1]
    users, beams = parents.shape[1], parents.shape[2]
    count = lax.axis_size("rows")
    device = lax.axis_index("rows")
    member, user = device % 4, device // 4
    slots = 16 * ((row_local + 3 * CAP + 15) // 16)

    split = (heads * AHEAD // 16, heads * BEHIND // 16)
    middle = heads * MIDDLE // 16
    early = sum(split)
    cuts = ((0, early), (early, middle), (early + middle, heads - early - middle))
    one, far, two, three, local_columns = gather(
        cuts[1], parents, token_ids, states, embed_table
    )
    qkv, piece_a, got_one = inputs(
        local_columns, jnp.transpose(qkv_weight, (1, 0, 2)), far, one, count, beams, split
    )
    two, three, qkv, lists = lax.optimization_barrier((two, three, qkv, parents[0]))
    got_two = swap(two, 2)
    got_three = swap(three, 3)
    qkv = qkv.reshape(count, beams, 3 * column_local)

    owner_block = lists // row_local
    blocks = owner_block.reshape(users, 4, row_local)
    at = jnp.arange(row_local, dtype=jnp.int32)
    same = (blocks[..., :, None] == blocks[..., None, :]) & (at[:, None] > at[None, :])
    rank = jnp.sum(same.astype(jnp.int32), axis=-1)
    offset = jnp.bitwise_xor(blocks, jnp.arange(4, dtype=jnp.int32)[None, :, None])
    slot = jnp.where(offset == 0, at[None, None, :], row_local + (offset - 1) * CAP + rank)
    slot = slot.reshape(users, beams)
    my_list = lax.dynamic_index_in_dim(lists, user, 0, keepdims=False)
    my_slot = lax.dynamic_index_in_dim(slot, user, 0, keepdims=False)
    held = my_list // row_local == member
    within = my_list % row_local
    slot_pick = held[None, :] & (my_slot[None, :] == jnp.arange(slots, dtype=jnp.int32)[:, None])
    owner = (held[:, None] & (within[:, None] == at[None, :])).astype(jnp.float32)
    own_slot = lax.dynamic_slice_in_dim(my_slot, member * row_local, row_local, 0)
    own_within = lax.dynamic_slice_in_dim(within, member * row_local, row_local, 0)
    far_row = own_slot >= row_local
    kind = jnp.where(far_row, (own_slot - row_local) // CAP + 1, 0)
    index = jnp.where(far_row, (own_slot - row_local) % CAP, own_within)
    source = (
        (jnp.arange(users, dtype=jnp.int32)[:, None] * 4 + owner_block) * slots + slot
    ).reshape(row_total)
    pick = (source[:, None] == jnp.arange(count * slots, dtype=jnp.int32)[None, :]).astype(
        jnp.bfloat16
    )

    normed = read(
        qkv, states, gate_weight, gate_bias, norm_gain, owner, slot_pick.astype(jnp.bfloat16)
    )
    mine = lax.dynamic_slice_in_dim(qkv, member * row_local, row_local, 1)
    keys = mine[:, :, head_size : 2 * head_size].astype(jnp.float32)
    values = jnp.swapaxes(mine[:, :, 2 * head_size :].astype(jnp.float32), 0, 1)
    logit = jnp.sum(keys * gate_weight[:, None, :], axis=-1) / math.sqrt(head_size)
    decay = jax.nn.sigmoid(logit + gate_bias[:, None]).T
    unit = keys * lax.rsqrt(jnp.sum(keys * keys, axis=-1, keepdims=True) + 1e-06)
    unit = jnp.swapaxes(unit, 0, 1)
    normed, pick, decay, unit, values, kind, index = lax.optimization_barrier(
        (normed, pick, decay, unit, values, kind, index)
    )
    every_normed, piece_c = spread_normed(normed, far, count, *cuts[2])
    ordered = jnp.dot(pick, every_normed, preferred_element_type=jnp.float32)
    attention = jnp.dot(
        ordered.astype(jnp.bfloat16), out_weight, preferred_element_type=jnp.float32
    )
    layer_out = (local_columns.astype(jnp.float32) + attention).astype(jnp.bfloat16)
    state_now = update(
        cuts, kind, index, decay, states,
        (got_one, got_two, got_three, piece_a, piece_c), unit, values
    )
    return (layer_out[None], state_now)


def from_partner(block, axis, stride):
    count = lax.axis_size(axis)
    route = []
    for low in range(count):
        high = low | 1 << stride
        if high != low and high < count:
            route += [(low, high), (high, low)]
    return lax.ppermute(block, axis, route)


def outgoing(state_now, parent_list, member, row_local, partner):
    target = jnp.bitwise_xor(member, partner)
    children = lax.dynamic_slice_in_dim(parent_list, target * row_local, row_local, 0)
    needed = children // row_local == member
    rank_index = jnp.cumsum(needed.astype(jnp.int32)) - 1
    slot_ids = jnp.arange(CAP, dtype=jnp.int32)
    chosen = jnp.sum(
        jnp.where(
            needed[None, :] & (rank_index[None, :] == slot_ids[:, None]),
            (children % row_local)[None, :],
            0,
        ),
        axis=1,
    )
    return jnp.take(state_now, chosen, axis=0)


def route(state_now, parent_list, member, row_local):
    first_out = outgoing(state_now, parent_list, member, row_local, 1)
    second_out = outgoing(state_now, parent_list, member, row_local, 2)
    corner_out = outgoing(state_now, parent_list, member, row_local, 3)
    got_one = from_partner(first_out, "rows", 0)
    got_two = from_partner(second_out, "rows", 1)
    relayed = from_partner(corner_out, "rows", 0)
    got_three = from_partner(relayed, "rows", 1)
    own_list = lax.dynamic_slice_in_dim(parent_list, member * row_local, row_local, 0)
    source = own_list // row_local
    partner = jnp.bitwise_xor(source, member)
    slot_index = jnp.arange(row_local, dtype=jnp.int32)
    earlier = (source[:, None] == source[None, :]) & (slot_index[:, None] > slot_index[None, :])
    rank_index = jnp.sum(earlier.astype(jnp.int32), axis=1)
    position = jnp.where(
        partner == 0, own_list % row_local, row_local + (partner - 1) * CAP + rank_index
    )
    pooled = jnp.concatenate([state_now, got_one, got_two, got_three], 0)
    return jnp.take(pooled, position, axis=0)


def per_device(
    token_ids,
    parents,
    states,
    embed_table,
    qkv_weight,
    gate_weight,
    gate_bias,
    norm_gain,
    out_weight,
):
    row_local = states.shape[0]
    heads = states.shape[1]
    head_size = states.shape[2]
    count = lax.axis_size("rows")
    if (
        embed_table.shape[1] == head_size
        and head_size % 128 == 0
        and count == heads
        and parents.shape[0] == 1
        and parents.shape[2] == 4 * row_local
        and parents.shape[1] * 4 == count
        and parents.shape[2] % 16 == 0
    ):
        return fast(
            token_ids, parents, states, embed_table, qkv_weight, gate_weight, gate_bias,
            norm_gain, out_weight
        )
    width = heads * head_size
    column_local = embed_table.shape[1]
    row_total = token_ids.shape[1]
    device = lax.axis_index("rows")
    member = device % 4
    user_index = device // 4
    weight_flat = qkv_weight.reshape(qkv_weight.shape[0], 3 * column_local)
    local_columns = jnp.take(embed_table, token_ids, axis=0)
    every_proj = jnp.einsum(
        "...rc,cf->...rf",
        lax.all_gather(local_columns, "rows", axis=2, tiled=True),
        weight_flat,
        preferred_element_type=jnp.float32,
    )
    state_now = states
    step_proj = every_proj[0]
    projected = step_proj.astype(jnp.bfloat16).reshape(row_total, 3, column_local)
    mine = lax.all_to_all(projected, "rows", split_axis=0, concat_axis=2, tiled=True)
    queries = mine[:, 0].reshape(row_local, heads, head_size)
    key_float = mine[:, 1].reshape(row_local, heads, head_size).astype(jnp.float32)
    values = mine[:, 2].reshape(row_local, heads, head_size).astype(jnp.float32)
    gate_logit = jnp.sum(key_float * gate_weight, axis=-1) / math.sqrt(head_size) + gate_bias
    decay_rate = jax.nn.sigmoid(gate_logit)
    key_unit = key_float * lax.rsqrt(jnp.sum(key_float * key_float, axis=-1, keepdims=True) + 1e-06)
    parent_list = lax.dynamic_index_in_dim(parents[0], user_index, 0, keepdims=False)
    prior_state = route(state_now, parent_list, member, row_local)
    new_state = (
        decay_rate[:, :, None, None] * prior_state.astype(jnp.float32)
        + key_unit[:, :, :, None] * values[:, :, None, :]
    )
    state_now = new_state.astype(jnp.bfloat16)
    readout = jnp.einsum("rhd,rhde->rhe", queries, state_now, preferred_element_type=jnp.float32)
    scaled = readout * lax.rsqrt(jnp.mean(readout * readout, axis=-1, keepdims=True) + 1e-05)
    normed = (scaled.reshape(row_local, width) * norm_gain).astype(jnp.bfloat16)
    attention = jnp.dot(
        lax.all_gather(normed, "rows", axis=0, tiled=True),
        out_weight,
        preferred_element_type=jnp.float32,
    )
    outputs = [(local_columns[0].astype(jnp.float32) + attention).astype(jnp.bfloat16)]
    return (jnp.stack(outputs), state_now)


def solution(mesh):
    placed = (
        P(None, "groups"),
        P(None, "groups", None),
        P(("groups", "rows"), None, None, None),
        P(None, "rows"),
        P(None, None, "rows"),
        P(),
        P(),
        P(),
        P(None, "rows"),
    )
    return jax.shard_map(
        per_device,
        mesh=mesh,
        in_specs=placed,
        out_specs=(P(None, "groups", "rows"), P(("groups", "rows"), None, None, None)),
        check_vma=False,
    )
```
